512 devices in a mesh: leaf: 64 (over y, z_lo, core), node: 8 (over z_hi, x).
Axes of the slice: x: 4, y: 8, z: 8 (z_hi: 2, z_lo: 4; z = z_hi * 4 + z_lo), core: 2. Of those that a mesh axis runs over, the one named last changes fastest.
Arguments:
- leaf_rhs: bfloat16 [64, 512, 128], P('leaf', 'node'), may hold values from -6 to 6
- leaf_inverse: bfloat16 [64, 512, 8192], P('leaf', 'node'), as said below
- leaf_update: bfloat16 [64, 1536, 512], P('leaf', None, 'node'), may hold values from -0.0625 to 0.0625
- root_tiles: int32 [4, 12], replicated, may hold values from 0 to 23, all different within a row
- leaf_dinv: float32 [64, 512], P('leaf', 'node'), may hold values from 0.5 to 2
- leaf_doff: float32 [64, 256], P('leaf', 'node'), may hold values from -0.5 to 0.5
- leaf_pairs: int32 [64, 256], P('leaf', 'node'), may hold values 0 or 1
- root_rhs: bfloat16 [3072, 128], P(('leaf', 'node')), may hold values from -6 to 6
- root_inverse: bfloat16 [3072, 3072], P(('leaf', 'node')), as said below
- root_dinv: float32 [3072], P(('leaf', 'node')), may hold values from 0.5 to 2
- root_doff: float32 [1536], P(('leaf', 'node')), may hold values from -0.5 to 0.5
- root_pairs: int32 [1536], P(('leaf', 'node')), may hold values 0 or 1
Outputs:
- leaf_solution: bfloat16 [64, 512, 128], P('leaf', 'node')
- root_solution: bfloat16 [3072, 128], P(('leaf', 'node'))
The draws below stay inside these ranges and needn't reach their ends.
Inputs may be any that keep to these rules, and one draw needn't show every extreme that they name: `leaf_inverse`: the 16 row blocks of each leaf, stacked, form Q M transpose(Q) for a permutation matrix Q and a unit lower triangular matrix M. root_inverse is unit lower triangular. `root_tiles`: the 12 tiles of one leaf are distinct, and every root tile is named by some leaf.
All inputs are finite; a program needn't handle non-finite values. No bound on the sum of `leaf_pairs` or of `root_pairs` on one device may be relied on, other than what follows from the above.
Results may differ from the reference program's by a relative error of at most 0.013.
Values may be sent and summed in bfloat16 or wider, within the bound.
No kernel may reach another device: no remote copies, remote signals or barrier semaphores. Data moves between devices by JAX's collectives and lax.ppermute only.
A program may use at most 64 MiB of HBM per device.

```python
import math
import jax
import jax.numpy as jnp
from jax import lax

LEAF_ROWS = 8192
RHS = 128
LEAVES = 4
ROOT_TILES = 24
LEAF_TILES = 12
SPLIT = 16
ROOT_ROWS = 3072


def unit_lower(key, shape, order):
    noise = jax.random.normal(key, shape, jnp.float32)
    lower = jnp.tril(noise * (0.5 / math.sqrt(order)), -1) + jnp.eye(order, dtype=jnp.float32)
    return lower


def permuted_leaf(key, index):
    matrix = unit_lower(jax.random.fold_in(key, 2 * index + 1), (LEAF_ROWS, LEAF_ROWS), LEAF_ROWS)
    order_key = jax.random.fold_in(key, 2 * index + 2)
    order = jax.random.permutation(order_key, jnp.arange(LEAF_ROWS, dtype=jnp.int32))
    return matrix[order][:, order]


def draw_leaf_inverse(key, part):
    base = jax.random.fold_in(key, 11)
    whole = jnp.stack([permuted_leaf(base, index) for index in range(LEAVES)], 0)
    return whole.astype(jnp.bfloat16).reshape(LEAVES * SPLIT, LEAF_ROWS // SPLIT, LEAF_ROWS)


def draw_root_inverse(key, part):
    return unit_lower(jax.random.fold_in(key, 23), (ROOT_ROWS, ROOT_ROWS), ROOT_ROWS).astype(jnp.bfloat16)


def touch_ends(entries, stream_key, least, high):
    longest = entries.shape.index(max(entries.shape))
    spots = []
    for shift in (0, 1):
        where = [jax.random.randint(jax.random.fold_in(stream_key, axis), (), 0, length) for axis, length in enumerate(entries.shape)]
        where[longest] = (where[longest] + shift) % entries.shape[longest]
        spots.append(tuple(where))
    return entries.at[spots[0]].set(least).at[spots[1]].set(high)


def steps_of(key, shape, split, smallest, high):
    gain = 1.0
    for dim, blocks in split:
        steps = jax.random.uniform(jax.random.fold_in(jax.random.fold_in(key, 6), dim), (blocks,), jnp.float32, smallest / len(split), high / len(split))
        gain = gain * jnp.repeat(jnp.exp(steps), shape[dim] // blocks).reshape((-1,) + (1,) * (len(shape) - 1 - dim))
    return gain


def different_ones(rng, rows, count, top, lift):
    sequence = jax.random.permutation(jax.random.fold_in(rng, 1), count)
    favour = sequence
    for power in range(3):
        favour = favour * favour // count
    favour = favour * lift // count
    lots = jax.random.randint(jax.random.fold_in(rng, 2), (rows, count), 0, 4096) + favour
    fixed_rows = jax.random.permutation(jax.random.fold_in(rng, 3), rows)[jnp.arange(count) % rows]
    lots = jnp.where(jnp.arange(rows)[:, None] == fixed_rows[None, :], 1 << 14, lots)
    score = lots * count + jnp.arange(count)
    return lax.top_k(score.astype(jnp.int32), top)[1].astype(jnp.int32)


def centred(stream_key, shape, spread, bound, shards=(), kind=jnp.bfloat16):
    entries = spread * jax.random.normal(stream_key, shape, jnp.float32)
    if shards:
        entries = entries * steps_of(stream_key, shape, shards, -0.22, 0.18)
    return jnp.clip(entries, -bound, bound).astype(kind)


def setup_inputs(seed: int = 0) -> dict:
    splits = jax.random.split(jax.random.key(seed), 13)
    return {
        "leaf_rhs": centred(splits[0], (LEAVES * SPLIT, LEAF_ROWS // SPLIT, RHS), 1.0, 6.0, ((0, 64), (1, 8))),
        "leaf_inverse": draw_leaf_inverse(jax.random.fold_in(splits[12], 71), 0),
        "leaf_update": centred(splits[2], (LEAVES * SPLIT, LEAF_TILES * 128, LEAF_ROWS // SPLIT), LEAF_ROWS ** -0.5, 0.0625, ((0, 64), (2, 8))),
        "root_tiles": different_ones(splits[3], LEAVES, ROOT_TILES, LEAF_TILES, 0),
        "leaf_dinv": jnp.clip(jnp.exp(math.log(2.0) - 1.3862944 * jax.random.uniform(splits[4], (LEAVES * SPLIT, LEAF_ROWS // SPLIT), jnp.float32) ** steps_of(splits[4], (LEAVES * SPLIT, LEAF_ROWS // SPLIT), ((0, 64), (1, 8)), -0.2, 0.2)), 0.5, 2.0),
        "leaf_doff": jnp.clip(jax.random.uniform(splits[5], (LEAVES * SPLIT, LEAF_ROWS // (2 * SPLIT)), jnp.float32, -0.5, 0.5) * steps_of(splits[5], (LEAVES * SPLIT, LEAF_ROWS // (2 * SPLIT)), ((0, 64), (1, 8)), -0.4, 0.0), -0.5, 0.5),
        "leaf_pairs": touch_ends((jax.random.randint(splits[6], (LEAVES * SPLIT, LEAF_ROWS // (2 * SPLIT)), 0, 2) < 1).astype(jnp.int32), jax.random.fold_in(splits[6], 1), 0, 1),
        "root_rhs": centred(splits[7], (ROOT_ROWS, RHS), 1.0, 6.0, ((0, 512),)),
        "root_inverse": draw_root_inverse(jax.random.fold_in(splits[12], 71), 0),
        "root_dinv": jnp.clip(jnp.exp(math.log(2.0) - 1.3862944 * jax.random.uniform(splits[9], (ROOT_ROWS,), jnp.float32) ** steps_of(splits[9], (ROOT_ROWS,), ((0, 512),), -0.2, 0.2)), 0.5, 2.0),
        "root_doff": jnp.clip(jax.random.uniform(splits[10], (ROOT_ROWS // 2,), jnp.float32, -0.5, 0.5) * steps_of(splits[10], (ROOT_ROWS // 2,), ((0, 512),), -0.4, 0.0), -0.5, 0.5),
        "root_pairs": touch_ends((jax.random.randint(splits[11], (ROOT_ROWS // 2,), 0, 2) < 1).astype(jnp.int32), jax.random.fold_in(splits[11], 1), 0, 1),
    }


tile_rows = 128


def pivot_solve(values, diagonal, coupling, pairs):
    length = values.shape[0]
    halves = values.reshape(length // 2, 2, values.shape[1])
    diag_two = diagonal.reshape(length // 2, 2)
    joined = (coupling * pairs.astype(jnp.float32))[:, None]
    first_row = diag_two[:, 0:1] * halves[:, 0, :] + joined * halves[:, 1, :]
    second_row = joined * halves[:, 0, :] + diag_two[:, 1:2] * halves[:, 1, :]
    return jnp.stack([first_row, second_row], axis=1).reshape(length, values.shape[1])


def tile_onehot(tile_ids):
    return (jnp.arange(ROOT_TILES, dtype=jnp.int32)[:, None] == tile_ids[None, :]).astype(jnp.float32)


def reference(leaf_rhs, leaf_inverse, leaf_update, root_tiles, leaf_dinv, leaf_doff, leaf_pairs, root_rhs, root_inverse, root_dinv, root_doff, root_pairs):
    full_rhs = leaf_rhs.reshape(LEAVES, LEAF_ROWS, RHS)
    full_inverse = leaf_inverse.reshape(LEAVES, LEAF_ROWS, LEAF_ROWS)
    full_update = leaf_update.reshape(LEAVES, SPLIT, LEAF_TILES * tile_rows, LEAF_ROWS // SPLIT)
    full_update = jnp.transpose(full_update, (0, 2, 1, 3)).reshape(LEAVES, LEAF_TILES * tile_rows, LEAF_ROWS)
    full_dinv = leaf_dinv.reshape(LEAVES, LEAF_ROWS)
    full_doff = leaf_doff.reshape(LEAVES, LEAF_ROWS // 2)
    full_pairs = leaf_pairs.reshape(LEAVES, LEAF_ROWS // 2)

    def forward_step(total, items):
        right, factor, update, tile_ids = items
        forward = jnp.dot(factor, right, preferred_element_type=jnp.float32).astype(jnp.bfloat16)
        update_term = jnp.dot(update, forward, preferred_element_type=jnp.float32)
        placed = jnp.einsum("tk,kar->tar", tile_onehot(tile_ids), update_term.reshape(LEAF_TILES, tile_rows, RHS), precision=lax.Precision.HIGHEST)
        return total + placed.reshape(ROOT_ROWS, RHS), forward

    gathered, leaf_forward = lax.scan(forward_step, jnp.zeros((ROOT_ROWS, RHS), jnp.float32), (full_rhs, full_inverse, full_update, root_tiles))
    root_reduced = (root_rhs.astype(jnp.float32) - gathered).astype(jnp.bfloat16)
    root_forward = jnp.dot(root_inverse, root_reduced, preferred_element_type=jnp.float32)
    root_scaled = pivot_solve(root_forward, root_dinv, root_doff, root_pairs).astype(jnp.bfloat16)
    root_solution = jnp.dot(root_inverse.T, root_scaled, preferred_element_type=jnp.float32).astype(jnp.bfloat16)
    root_blocks = root_solution.astype(jnp.float32).reshape(ROOT_TILES, tile_rows, RHS)

    def backward_step(items):
        forward, factor, update, tile_ids, diagonal, coupling, pairs = items
        tile_values = jnp.einsum("tk,tar->kar", tile_onehot(tile_ids), root_blocks, precision=lax.Precision.HIGHEST)
        tile_values = tile_values.reshape(LEAF_TILES * tile_rows, RHS).astype(jnp.bfloat16)
        scaled = pivot_solve(forward.astype(jnp.float32), diagonal, coupling, pairs)
        leaf_vector = (scaled - jnp.dot(update.T, tile_values, preferred_element_type=jnp.float32)).astype(jnp.bfloat16)
        return jnp.dot(factor.T, leaf_vector, preferred_element_type=jnp.float32).astype(jnp.bfloat16)

    leaf_solution = lax.map(backward_step, (leaf_forward, full_inverse, full_update, root_tiles, full_dinv, full_doff, full_pairs))
    return leaf_solution.reshape(LEAVES * SPLIT, LEAF_ROWS // SPLIT, RHS), root_solution
```

```python
import jax
import jax.numpy as jnp
from jax import lax
from jax.experimental import pallas as pl
from jax.experimental.pallas import tpu as pltpu
from jax.sharding import Mesh
from jax.sharding import PartitionSpec as P

LEAVES = 4
ROOT_TILES = 24
LEAF_TILES = 12
TILE = 128
RHS = 128
ROOT_ROWS = ROOT_TILES * TILE
LEAF_ROWS = 8192

AXES = ("p", "yl", "zl", "c", "zh", "x")
SIZES = (4, 2, 4, 2, 2, 4)
LEAF = ("p", "yl", "zl", "c")
NODE = ("zh", "x")
CX = ("c", "x")
YZ = ("yl", "zl", "zh")
YALL = ("p", "yl")
Q = ("zl", "c", "zh", "x")
GRAN = ("c", "zl", "zh")
XGRAN = ("x", "c", "zl", "zh")
PYX = ("p", "yl", "x")

F32 = jnp.float32
BF16 = jnp.bfloat16


def exchange(blocks, axes):
    return lax.all_to_all(blocks, axes, 0, 0)


def gather(value, axes):
    count = 1
    for axis in axes:
        count *= lax.axis_size(axis)
    return exchange(jnp.broadcast_to(value[None], (count,) + value.shape), axes)


def summed(blocks):
    return jnp.sum(blocks.astype(F32), axis=0)


def split_columns_kernel(source_ref, out_ref):
    lane = lax.broadcasted_iota(jnp.int32, (64, TILE), 1)
    low = lane < 64
    for m in range(8):
        for core in range(2):
            for xh in range(2):
                first = ((m * 2 + core) * 2) * 2 + xh
                second = first + 2
                a = source_ref[:, first * TILE : (first + 1) * TILE].astype(F32)
                b = source_ref[:, second * TILE : (second + 1) * TILE].astype(F32)
                even = jnp.where(low, a, pltpu.roll(b, 64, 1))
                odd = jnp.where(low, pltpu.roll(a, 64, 1), b)
                place = slice(m * TILE, (m + 1) * TILE)
                out_ref[core * 4 + xh * 2, :, place] = even.astype(BF16)
                out_ref[core * 4 + xh * 2 + 1, :, place] = odd.astype(BF16)


def split_columns(factor_rows):
    return pl.pallas_call(
        split_columns_kernel,
        out_shape=jax.ShapeDtypeStruct((8, 64, 1024), BF16),
    )(factor_rows)


def combine_kernel(tiles_ref, terms_ref, rhs_ref, out_ref, total_ref):
    total_ref[...] = jnp.zeros_like(total_ref)
    for p in range(LEAVES):
        for k in range(LEAF_TILES):
            tile = tiles_ref[p, k]
            term = terms_ref[p * 24 + k].astype(F32) + terms_ref[p * 24 + 12 + k].astype(F32)
            total_ref[tile] = total_ref[tile] + term
    out_ref[...] = (rhs_ref[...].astype(F32) - total_ref[...]).astype(BF16)


def combine(root_tiles, terms, rhs):
    return pl.pallas_call(
        combine_kernel,
        out_shape=jax.ShapeDtypeStruct((ROOT_TILES, 8, RHS), BF16),
        in_specs=[
            pl.BlockSpec(memory_space=pltpu.SMEM),
            pl.BlockSpec(memory_space=pltpu.VMEM),
            pl.BlockSpec(memory_space=pltpu.VMEM),
        ],
        out_specs=pl.BlockSpec(memory_space=pltpu.VMEM),
        scratch_shapes=[pltpu.VMEM((ROOT_TILES, 8, RHS), F32)],
    )(root_tiles, terms, rhs)


def pivot_solve(values, diagonal, joined):
    length = values.shape[0]
    halves = values.reshape(length // 2, 2, values.shape[1])
    swapped = halves[:, ::-1, :].reshape(length, values.shape[1])
    return diagonal * values + joined * swapped


def parts_of(value):
    high = lax.reduce_precision(value, 8, 7)
    rest = value - high
    middle = lax.reduce_precision(rest, 8, 7)
    low = lax.reduce_precision(rest - middle, 8, 7)
    return [high, middle, low]


def transposed_product(matrix, vector):
    return lax.dot_general(
        matrix, vector, (((0,), (0,)), ((), ())), preferred_element_type=F32
    )


def on_device(
    leaf_rhs,
    leaf_inverse,
    leaf_update,
    root_tiles,
    leaf_dinv,
    leaf_doff,
    leaf_pairs,
    root_rhs,
    root_inverse,
    root_dinv,
    root_doff,
    root_pairs,
):
    blocks = exchange(split_columns(leaf_inverse[0]), CX).reshape(512, 1024)
    rhs_part = gather(leaf_rhs[0], YZ).reshape(1024, RHS)

    joined = jnp.repeat(root_doff * root_pairs.astype(F32), 2)
    columns = jnp.stack(parts_of(root_dinv) + parts_of(joined), axis=1).astype(BF16)
    columns = jnp.pad(columns, ((0, 0), (0, TILE - 6)))
    root_pack = jnp.concatenate([root_inverse, root_rhs, columns], axis=1)
    root_pack = gather(jnp.pad(root_pack, ((0, 2), (0, 0))), YALL).reshape(64, ROOT_ROWS + 2 * TILE)
    root_rows = root_pack[:, :ROOT_ROWS]
    pivots = root_pack[:, ROOT_ROWS + TILE :].astype(F32)
    dinv_rows = pivots[:, 0:1] + pivots[:, 1:2] + pivots[:, 2:3]
    joined_rows = pivots[:, 3:4] + pivots[:, 4:5] + pivots[:, 5:6]
    all_rhs = gather(root_pack[:, ROOT_ROWS : ROOT_ROWS + TILE], Q).reshape(64 * 64, RHS)
    granule = lax.axis_index(GRAN)
    at = jnp.arange(64 * 64, dtype=jnp.int32)
    held = jnp.where(at % 8 < 6, 384 * (at // 8 % 8) + 6 * (at // 64) + at % 8, -1)
    want = jnp.arange(ROOT_TILES * 8, dtype=jnp.int32)
    want = TILE * (want // 8) + 8 * granule + want % 8
    select = (want[:, None] == held[None, :]).astype(BF16)
    rhs_rows = jnp.dot(select, all_rhs, preferred_element_type=F32).astype(BF16)
    rhs_rows = rhs_rows.reshape(ROOT_TILES, 8, RHS)

    partial = jnp.dot(blocks, rhs_part, preferred_element_type=F32).astype(BF16)
    leaf_forward = summed(exchange(partial.reshape(8, 64, RHS), CX)).astype(BF16)

    update = leaf_update[0]
    ordered = update.reshape(4, 3, 16, 8, 64).transpose(0, 2, 1, 3, 4).reshape(1536, 64)
    term = jnp.dot(ordered, leaf_forward, preferred_element_type=F32).astype(BF16)
    term = summed(exchange(term.reshape(64, 24, RHS), XGRAN)).astype(BF16)
    terms = gather(term, PYX).reshape(96, 8, RHS)
    reduced = combine(root_tiles, terms, rhs_rows)
    reduced = gather(reduced, GRAN).transpose(1, 0, 2, 3).reshape(ROOT_ROWS, RHS)

    root_forward = jnp.dot(root_rows, reduced, preferred_element_type=F32)
    root_scaled = pivot_solve(root_forward, dinv_rows, joined_rows).astype(BF16)
    back = transposed_product(root_rows, root_scaled).astype(BF16)
    root_part = summed(exchange(back.reshape(64, 48, RHS), Q)).astype(BF16)
    root_full = gather(root_part, Q).reshape(ROOT_ROWS, RHS)
    root_own = lax.dynamic_slice_in_dim(root_full, lax.axis_index(AXES) * 6, 6, 0)

    tile_ids = lax.dynamic_index_in_dim(root_tiles, lax.axis_index("p"), 0, keepdims=False)
    onehot = (tile_ids[:, None] == jnp.arange(ROOT_TILES, dtype=jnp.int32)[None, :]).astype(BF16)
    tile_values = jnp.einsum(
        "kt,tar->kar", onehot, root_full.reshape(ROOT_TILES, TILE, RHS), preferred_element_type=F32
    )
    tile_values = tile_values.astype(BF16).reshape(LEAF_TILES * TILE, RHS)
    coupling = transposed_product(update, tile_values)
    leaf_joined = jnp.repeat(leaf_doff[0] * leaf_pairs[0].astype(F32), 2)[:, None]
    scaled = pivot_solve(leaf_forward.astype(F32), leaf_dinv[0][:, None], leaf_joined)
    leaf_vector = (scaled - coupling).astype(BF16)
    vector = gather(leaf_vector, CX).reshape(512, RHS)
    back_leaf = transposed_product(blocks, vector).astype(BF16)
    leaf_solution = summed(exchange(back_leaf.reshape(16, 64, RHS), YZ)).astype(BF16)
    return (leaf_solution[None], root_own)


def solution(mesh):
    fine = Mesh(mesh.devices.reshape(SIZES), AXES)
    in_specs = (
        P(LEAF, NODE, None),
        P(LEAF, NODE, None),
        P(LEAF, None, NODE),
        P(),
        P(LEAF, NODE),
        P(LEAF, NODE),
        P(LEAF, NODE),
        P(AXES, None),
        P(AXES, None),
        P(AXES),
        P(AXES),
        P(AXES),
    )
    out_specs = (P(LEAF, NODE, None), P(AXES, None))
    return jax.shard_map(
        on_device, mesh=fine, in_specs=in_specs, out_specs=out_specs, check_vma=False
    )
```

```python
import jax
import jax.numpy as jnp
from jax import lax
from jax.experimental import pallas as pl
from jax.experimental.pallas import tpu as pltpu
from jax.sharding import Mesh
from jax.sharding import PartitionSpec as P

LEAVES = 4
ROOT_TILES = 24
LEAF_TILES = 12
TILE = 128
RHS = 128
ROOT_ROWS = ROOT_TILES * TILE
LEAF_ROWS = 8192

AXES = ("p", "yl", "zl", "c", "zh", "x")
SIZES = (4, 2, 4, 2, 2, 4)
LEAF = ("p", "yl", "zl", "c")
NODE = ("zh", "x")
CX = ("c", "x")
YZ = ("yl", "zl", "zh")
YALL = ("p", "yl")
Z = ("zl", "zh")
XZ = ("x", "zl", "zh")
ZX = ("zl", "zh", "x")
PYX = ("p", "yl", "x")

F32 = jnp.float32
BF16 = jnp.bfloat16


def exchange(blocks, axes):
    return lax.all_to_all(blocks, axes, 0, 0)


def gather(value, axes):
    count = 1
    for axis in axes:
        count *= lax.axis_size(axis)
    return exchange(jnp.broadcast_to(value[None], (count,) + value.shape), axes)


def summed(blocks):
    return jnp.sum(blocks.astype(F32), axis=0)


def split_columns_kernel(source_ref, out_ref):
    lane = lax.broadcasted_iota(jnp.int32, (64, TILE), 1)
    low = lane < 64
    for m in range(8):
        for core in range(2):
            for xh in range(2):
                first = ((m * 2 + core) * 2) * 2 + xh
                second = first + 2
                a = source_ref[:, first * TILE : (first + 1) * TILE].astype(F32)
                b = source_ref[:, second * TILE : (second + 1) * TILE].astype(F32)
                even = jnp.where(low, a, pltpu.roll(b, 64, 1))
                odd = jnp.where(low, pltpu.roll(a, 64, 1), b)
                place = slice(m * TILE, (m + 1) * TILE)
                out_ref[core * 4 + xh * 2, :, place] = even.astype(BF16)
                out_ref[core * 4 + xh * 2 + 1, :, place] = odd.astype(BF16)


def split_columns(factor_rows):
    return pl.pallas_call(
        split_columns_kernel,
        out_shape=jax.ShapeDtypeStruct((8, 64, 1024), BF16),
    )(factor_rows)


def combine_kernel(tiles_ref, terms_ref, out_ref, total_ref):
    for y in range(8):
        for x in range(3):
            total_ref[3 * y + x] = -terms_ref[(y * 4 + x) * 4 + 3].astype(F32)
    for p in range(LEAVES):
        for x in range(4):
            for k in range(3):
                tile = tiles_ref[p, 3 * x + k]
                first = (p * 8 + x) * 4 + k
                term = terms_ref[first].astype(F32) + terms_ref[first + 16].astype(F32)
                total_ref[tile] = total_ref[tile] + term
    out_ref[...] = (-total_ref[...]).astype(BF16)


def combine(root_tiles, terms):
    return pl.pallas_call(
        combine_kernel,
        out_shape=jax.ShapeDtypeStruct((ROOT_TILES, 8, RHS), BF16),
        in_specs=[
            pl.BlockSpec(memory_space=pltpu.SMEM),
            pl.BlockSpec(memory_space=pltpu.VMEM),
        ],
        out_specs=pl.BlockSpec(memory_space=pltpu.VMEM),
        scratch_shapes=[pltpu.VMEM((ROOT_TILES, 8, RHS), F32)],
    )(root_tiles, terms)


def pivot_solve(values, diagonal, joined):
    length = values.shape[0]
    halves = values.reshape(length // 2, 2, values.shape[1])
    swapped = halves[:, ::-1, :].reshape(length, values.shape[1])
    return diagonal * values + joined * swapped


def other_core(value):
    return lax.ppermute(value, "c", [(0, 1), (1, 0)])


def both_cores(value):
    other = other_core(value)
    first = lax.axis_index("c") == 0
    return jnp.where(first, jnp.stack([value, other]), jnp.stack([other, value]))


def gather_leaf_rhs(value):
    def doubled(held, axis, mask, low, place):
        pairs = [(i, i ^ mask) for i in range(lax.axis_size(axis))]
        other = lax.ppermute(held, axis, pairs)
        return jnp.where(low, jnp.stack([held, other], place), jnp.stack([other, held], place))

    zl = lax.axis_index("zl")
    held = doubled(value, "zh", 1, lax.axis_index("zh") == 0, 0)
    held = doubled(held, "zl", 2, zl < 2, 0)
    held = doubled(held, "zl", 1, zl % 2 == 0, 1)
    held = doubled(held, "yl", 1, lax.axis_index("yl") == 0, 0)
    return held.reshape(1024, RHS)


def transposed_product(matrix, vector):
    return lax.dot_general(
        matrix, vector, (((0,), (0,)), ((), ())), preferred_element_type=F32
    )


def on_device(
    leaf_rhs,
    leaf_inverse,
    leaf_update,
    root_tiles,
    leaf_dinv,
    leaf_doff,
    leaf_pairs,
    root_rhs,
    root_inverse,
    root_dinv,
    root_doff,
    root_pairs,
):
    blocks = exchange(split_columns(leaf_inverse[0]), CX).reshape(512, 1024)
    rhs_part = gather_leaf_rhs(leaf_rhs[0])
    partial = jnp.dot(blocks, rhs_part, preferred_element_type=F32).astype(BF16)
    leaf_forward = summed(exchange(partial.reshape(8, 64, RHS), CX)).astype(BF16)

    update = leaf_update[0]
    ordered = update.reshape(4, 3, 2, 8, 8, 64).transpose(2, 0, 3, 1, 4, 5).reshape(64, 24, 64)
    chunk = jnp.arange(512, dtype=jnp.int32)
    place = chunk // 8
    x_of = place // 8 % 4
    tile_row = 8 * (place // 32 * 8 + place % 8) + chunk % 8
    row = TILE * (3 * lax.axis_index(YALL) + x_of) + tile_row
    row = jnp.where(x_of < 3, row, -1) - 6 * lax.axis_index(AXES)
    select = (row[:, None] == jnp.arange(8, dtype=jnp.int32)[None, :]) & (row < 6)[:, None]
    select = select.astype(BF16).reshape(64, 8, 8)
    left = jnp.concatenate(
        [jnp.pad(ordered, ((0, 0), (0, 0), (0, 8))), jnp.pad(select, ((0, 0), (0, 0), (64, 0)))], 1
    ).reshape(2048, 72)
    right = jnp.concatenate([leaf_forward, jnp.pad(root_rhs, ((0, 2), (0, 0)))], 0)
    term = jnp.dot(left, right, preferred_element_type=F32).astype(BF16)
    term = summed(exchange(term.reshape(2, 1024, RHS), ("c",))).astype(BF16)
    term = summed(exchange(term.reshape(32, 32, RHS), XZ)).astype(BF16)
    reduced = combine(root_tiles, gather(term, PYX).reshape(128, 8, RHS))
    reduced = both_cores(gather(reduced, Z)).reshape(16, ROOT_TILES, 8, RHS)
    reduced = reduced.transpose(1, 0, 2, 3).reshape(ROOT_ROWS, RHS)

    root_forward = jnp.dot(root_inverse, reduced, preferred_element_type=F32)
    joined = jnp.repeat(root_doff * root_pairs.astype(F32), 2)[:, None]
    root_scaled = pivot_solve(root_forward, root_dinv[:, None], joined).astype(BF16)
    back = transposed_product(root_inverse, root_scaled).astype(BF16)
    back = summed(exchange(back.reshape(2, ROOT_ROWS // 2, RHS), ("c",))).astype(BF16)
    back = summed(exchange(back.reshape(32, 48, RHS), ZX)).astype(BF16)
    root_part = summed(gather(back, YALL)).astype(BF16)
    root_full = both_cores(gather(root_part, ZX)).reshape(ROOT_ROWS, RHS)
    root_own = lax.dynamic_slice_in_dim(root_full, lax.axis_index(AXES) * 6, 6, 0)

    tile_ids = lax.dynamic_index_in_dim(root_tiles, lax.axis_index("p"), 0, keepdims=False)
    onehot = (tile_ids[:, None] == jnp.arange(ROOT_TILES, dtype=jnp.int32)[None, :]).astype(BF16)
    tile_values = jnp.einsum(
        "kt,tar->kar", onehot, root_full.reshape(ROOT_TILES, TILE, RHS), preferred_element_type=F32
    )
    tile_values = tile_values.astype(BF16).reshape(LEAF_TILES * TILE, RHS)
    coupling = transposed_product(update, tile_values)
    leaf_joined = jnp.repeat(leaf_doff[0] * leaf_pairs[0].astype(F32), 2)[:, None]
    scaled = pivot_solve(leaf_forward.astype(F32), leaf_dinv[0][:, None], leaf_joined)
    leaf_vector = (scaled - coupling).astype(BF16)
    vector = gather(leaf_vector, CX).reshape(512, RHS)
    back_leaf = transposed_product(blocks, vector).astype(BF16)
    leaf_solution = summed(exchange(back_leaf.reshape(16, 64, RHS), YZ)).astype(BF16)
    return (leaf_solution[None], root_own)


def solution(mesh):
    fine = Mesh(mesh.devices.reshape(SIZES), AXES)
    in_specs = (
        P(LEAF, NODE, None),
        P(LEAF, NODE, None),
        P(LEAF, None, NODE),
        P(),
        P(LEAF, NODE),
        P(LEAF, NODE),
        P(LEAF, NODE),
        P(AXES, None),
        P(AXES, None),
        P(AXES),
        P(AXES),
        P(AXES),
    )
    out_specs = (P(LEAF, NODE, None), P(AXES, None))
    return jax.shard_map(
        on_device, mesh=fine, in_specs=in_specs, out_specs=out_specs, check_vma=False
    )
```

```python
import jax
import jax.numpy as jnp
from jax import lax
from jax.experimental import pallas as pl
from jax.experimental.pallas import tpu as pltpu
from jax.sharding import Mesh
from jax.sharding import PartitionSpec as P

LEAVES = 4
ROOT_TILES = 24
LEAF_TILES = 12
TILE = 128
RHS = 128
ROOT_ROWS = ROOT_TILES * TILE
LEAF_ROWS = 8192

AXES = ("p", "yl", "zl", "c", "zh", "x")
SIZES = (4, 2, 4, 2, 2, 4)
LEAF = ("p", "yl", "zl", "c")
NODE = ("zh", "x")
CX = ("c", "x")
YZ = ("yl", "zl", "zh")
YALL = ("p", "yl")
Z = ("zl", "zh")
GRAN = ("c", "zl", "zh")
ZX = ("zl", "zh", "x")

F32 = jnp.float32
BF16 = jnp.bfloat16


def exchange(blocks, axes):
    return lax.all_to_all(blocks, axes, 0, 0)


def gather(value, axes):
    count = 1
    for axis in axes:
        count *= lax.axis_size(axis)
    return exchange(jnp.broadcast_to(value[None], (count,) + value.shape), axes)


def summed(blocks):
    return jnp.sum(blocks.astype(F32), axis=0)


def split_columns_kernel(source_ref, out_ref):
    lane = lax.broadcasted_iota(jnp.int32, (64, TILE), 1)
    low = lane < 64
    for m in range(8):
        for core in range(2):
            for xh in range(2):
                first = ((m * 2 + core) * 2) * 2 + xh
                second = first + 2
                a = source_ref[:, first * TILE : (first + 1) * TILE].astype(F32)
                b = source_ref[:, second * TILE : (second + 1) * TILE].astype(F32)
                even = jnp.where(low, a, pltpu.roll(b, 64, 1))
                odd = jnp.where(low, pltpu.roll(a, 64, 1), b)
                place = slice(m * TILE, (m + 1) * TILE)
                out_ref[core * 4 + xh * 2, :, place] = even.astype(BF16)
                out_ref[core * 4 + xh * 2 + 1, :, place] = odd.astype(BF16)


def split_columns(factor_rows):
    return pl.pallas_call(
        split_columns_kernel,
        out_shape=jax.ShapeDtypeStruct((8, 64, 1024), BF16),
    )(factor_rows)


def combine_kernel(tiles_ref, terms_ref, out_ref, total_ref):
    for y in range(8):
        for j in range(3):
            total_ref[3 * y + j] = -terms_ref[15 * y + 12 + j].astype(F32)
    for p in range(LEAVES):
        for k in range(LEAF_TILES):
            tile = tiles_ref[p, k]
            term = terms_ref[30 * p + k].astype(F32) + terms_ref[30 * p + 15 + k].astype(F32)
            total_ref[tile] = total_ref[tile] + term
    out_ref[...] = (-total_ref[...]).astype(BF16)


def combine(root_tiles, terms):
    return pl.pallas_call(
        combine_kernel,
        out_shape=jax.ShapeDtypeStruct((ROOT_TILES, 8, RHS), BF16),
        in_specs=[
            pl.BlockSpec(memory_space=pltpu.SMEM),
            pl.BlockSpec(memory_space=pltpu.VMEM),
        ],
        out_specs=pl.BlockSpec(memory_space=pltpu.VMEM),
        scratch_shapes=[pltpu.VMEM((ROOT_TILES, 8, RHS), F32)],
    )(root_tiles, terms)


def granule_columns_kernel(source_ref, pivots_ref, out_ref):
    slot = lax.broadcasted_iota(jnp.int32, (8, TILE), 1) // 8
    tiles = [source_ref[:, t * TILE : (t + 1) * TILE].astype(F32) for t in range(ROOT_TILES)]
    for a in range(16):
        first = tiles[0] * 0.0
        second = pivots_ref[...]
        for t in range(16):
            first = jnp.where(slot == t, pltpu.roll(tiles[t], (t - a) * 8 % TILE, 1), first)
        for t in range(8):
            second = jnp.where(slot == t, pltpu.roll(tiles[16 + t], (t - a) * 8 % TILE, 1), second)
        out_ref[a, :, :TILE] = first.astype(BF16)
        out_ref[a, :, TILE:] = second.astype(BF16)


def granule_columns(rows, pivots):
    return pl.pallas_call(
        granule_columns_kernel,
        out_shape=jax.ShapeDtypeStruct((16, 8, 2 * TILE), BF16),
    )(rows, pivots)


def parts_of(value):
    high = lax.reduce_precision(value, 8, 7)
    rest = value - high
    middle = lax.reduce_precision(rest, 8, 7)
    low = lax.reduce_precision(rest - middle, 8, 7)
    return [high, middle, low]


def pivot_solve(values, diagonal, joined):
    length = values.shape[0]
    halves = values.reshape(length // 2, 2, values.shape[1])
    swapped = halves[:, ::-1, :].reshape(length, values.shape[1])
    return diagonal * values + joined * swapped


def other_core(value):
    return lax.ppermute(value, "c", [(0, 1), (1, 0)])


def both_cores(value):
    other = other_core(value)
    first = lax.axis_index("c") == 0
    return jnp.where(first, jnp.stack([value, other]), jnp.stack([other, value]))


def gather_leaf_rhs(value):
    def doubled(held, axis, mask, low, place):
        pairs = [(i, i ^ mask) for i in range(lax.axis_size(axis))]
        other = lax.ppermute(held, axis, pairs)
        return jnp.where(low, jnp.stack([held, other], place), jnp.stack([other, held], place))

    zl = lax.axis_index("zl")
    held = doubled(value, "zh", 1, lax.axis_index("zh") == 0, 0)
    held = doubled(held, "zl", 2, zl < 2, 0)
    held = doubled(held, "zl", 1, zl % 2 == 0, 1)
    held = doubled(held, "yl", 1, lax.axis_index("yl") == 0, 0)
    return held.reshape(1024, RHS)


def transposed_product(matrix, vector):
    return lax.dot_general(
        matrix, vector, (((0,), (0,)), ((), ())), preferred_element_type=F32
    )


def on_device(
    leaf_rhs,
    leaf_inverse,
    leaf_update,
    root_tiles,
    leaf_dinv,
    leaf_doff,
    leaf_pairs,
    root_rhs,
    root_inverse,
    root_dinv,
    root_doff,
    root_pairs,
):
    blocks = exchange(split_columns(leaf_inverse[0]), CX).reshape(512, 1024)
    rhs_part = gather_leaf_rhs(leaf_rhs[0])
    partial = jnp.dot(blocks, rhs_part, preferred_element_type=F32).astype(BF16)
    leaf_forward = summed(exchange(partial.reshape(8, 64, RHS), CX)).astype(BF16)

    joined = jnp.repeat(root_doff * root_pairs.astype(F32), 2)
    pivots = jnp.stack(parts_of(root_dinv) + parts_of(joined), axis=1)
    pivots = jnp.pad(pivots, ((0, 2), (64, TILE - 70)))
    root_block = granule_columns(jnp.pad(root_inverse, ((0, 2), (0, 0))), pivots)
    root_block = exchange(root_block, GRAN).reshape(128, 2 * TILE)
    pivots = root_block[:, 192:198].astype(F32)
    dinv_rows = pivots[:, 0:1] + pivots[:, 1:2] + pivots[:, 2:3]
    joined_rows = pivots[:, 3:4] + pivots[:, 4:5] + pivots[:, 5:6]
    root_block = root_block[:, :192]

    update = leaf_update[0]
    ordered = update.reshape(12, 16, 8, 64).transpose(1, 0, 2, 3).reshape(16, 96, 64)
    at = jnp.arange(16 * 24, dtype=jnp.int32)
    row = TILE * (3 * lax.axis_index(YALL) + at // 8 % 3) + 8 * (at // 24) + at % 8
    row = row - 6 * lax.axis_index(AXES)
    select = (row[:, None] == jnp.arange(8, dtype=jnp.int32)[None, :]) & (row < 6)[:, None]
    select = select.astype(BF16).reshape(16, 24, 8)
    left = jnp.concatenate(
        [jnp.pad(ordered, ((0, 0), (0, 0), (0, 8))), jnp.pad(select, ((0, 0), (0, 0), (64, 0)))], 1
    ).reshape(1920, 72)
    right = jnp.concatenate([leaf_forward, jnp.pad(root_rhs, ((0, 2), (0, 0)))], 0)
    term = jnp.dot(left, right, preferred_element_type=F32).astype(BF16)
    term = summed(exchange(term.reshape(2, 960, RHS), ("c",))).astype(BF16)
    term = summed(exchange(term.reshape(8, 120, RHS), Z)).astype(BF16)
    term = summed(gather(term, ("x",))).astype(BF16)
    reduced = combine(root_tiles, gather(term, YALL).reshape(120, 8, RHS)).reshape(192, RHS)

    forward = jnp.dot(root_block, reduced, preferred_element_type=F32)
    forward = forward + other_core(forward.astype(BF16)).astype(F32)
    forward = summed(gather(forward.astype(BF16), Z))
    root_scaled = pivot_solve(forward, dinv_rows, joined_rows).astype(BF16)
    back = transposed_product(root_block, root_scaled).astype(BF16)
    back = summed(exchange(back.reshape(4, 48, RHS), ("x",))).astype(BF16)
    root_part = summed(gather(back, YALL)).astype(BF16)
    root_full = both_cores(gather(root_part, ZX)).reshape(16, ROOT_TILES, 8, RHS)
    root_full = root_full.transpose(1, 0, 2, 3).reshape(ROOT_ROWS, RHS)
    root_own = lax.dynamic_slice_in_dim(root_full, lax.axis_index(AXES) * 6, 6, 0)

    tile_ids = lax.dynamic_index_in_dim(root_tiles, lax.axis_index("p"), 0, keepdims=False)
    onehot = (tile_ids[:, None] == jnp.arange(ROOT_TILES, dtype=jnp.int32)[None, :]).astype(BF16)
    tile_values = jnp.einsum(
        "kt,tar->kar", onehot, root_full.reshape(ROOT_TILES, TILE, RHS), preferred_element_type=F32
    )
    tile_values = tile_values.astype(BF16).reshape(LEAF_TILES * TILE, RHS)
    coupling = transposed_product(update, tile_values)
    leaf_joined = jnp.repeat(leaf_doff[0] * leaf_pairs[0].astype(F32), 2)[:, None]
    scaled = pivot_solve(leaf_forward.astype(F32), leaf_dinv[0][:, None], leaf_joined)
    leaf_vector = (scaled - coupling).astype(BF16)
    vector = gather(leaf_vector, CX).reshape(512, RHS)
    back_leaf = transposed_product(blocks, vector).astype(BF16)
    leaf_solution = summed(exchange(back_leaf.reshape(16, 64, RHS), YZ)).astype(BF16)
    return (leaf_solution[None], root_own)


def solution(mesh):
    fine = Mesh(mesh.devices.reshape(SIZES), AXES)
    in_specs = (
        P(LEAF, NODE, None),
        P(LEAF, NODE, None),
        P(LEAF, None, NODE),
        P(),
        P(LEAF, NODE),
        P(LEAF, NODE),
        P(LEAF, NODE),
        P(AXES, None),
        P(AXES, None),
        P(AXES),
        P(AXES),
        P(AXES),
    )
    out_specs = (P(LEAF, NODE, None), P(AXES, None))
    return jax.shard_map(
        on_device, mesh=fine, in_specs=in_specs, out_specs=out_specs, check_vma=False
    )
```

```python
import jax
import jax.numpy as jnp
from jax import lax
from jax.experimental import pallas as pl
from jax.experimental.pallas import tpu as pltpu
from jax.sharding import Mesh
from jax.sharding import PartitionSpec as P

LEAVES = 4
ROOT_TILES = 24
LEAF_TILES = 12
TILE = 128
RHS = 128
ROOT_ROWS = ROOT_TILES * TILE
LEAF_ROWS = 8192

AXES = ("p", "yl", "zl", "c", "zh", "x")
SIZES = (4, 2, 4, 2, 2, 4)
LEAF = ("p", "yl", "zl", "c")
NODE = ("zh", "x")
CX = ("c", "x")
YZ = ("yl", "zl", "zh")
YALL = ("p", "yl")
Z = ("zl", "zh")
ZX = ("zl", "zh", "x")


F32 = jnp.float32
BF16 = jnp.bfloat16


def exchange(blocks, axes):
    return lax.all_to_all(blocks, axes, 0, 0)


def gather(value, axes):
    count = 1
    for axis in axes:
        count *= lax.axis_size(axis)
    return exchange(jnp.broadcast_to(value[None], (count,) + value.shape), axes)


def summed(blocks):
    return jnp.sum(blocks.astype(F32), axis=0)


def split_columns_kernel(x_ref, source_ref, out_ref):
    own = x_ref[0]
    lane = lax.broadcasted_iota(jnp.int32, (64, TILE), 1)
    low = lane < 64
    for m in range(8):
        for core in range(2):
            for xh in range(2):
                first = ((m * 2 + core) * 2) * 2 + xh
                second = first + 2
                a = source_ref[:, first * TILE : (first + 1) * TILE].astype(F32)
                b = source_ref[:, second * TILE : (second + 1) * TILE].astype(F32)
                even = jnp.where(low, a, pltpu.roll(b, 64, 1))
                odd = jnp.where(low, pltpu.roll(a, 64, 1), b)
                place = slice(m * TILE, (m + 1) * TILE)
                out_ref[core, (xh * 2) ^ own, :, place] = even.astype(BF16)
                out_ref[core, (xh * 2 + 1) ^ own, :, place] = odd.astype(BF16)


SCALARS = pl.BlockSpec(memory_space=pltpu.SMEM)
VECTORS = pl.BlockSpec(memory_space=pltpu.VMEM)


def split_columns(own_x, factor_rows):
    return pl.pallas_call(
        split_columns_kernel,
        out_shape=jax.ShapeDtypeStruct((2, 4, 64, 1024), BF16),
        in_specs=[SCALARS, VECTORS],
        out_specs=VECTORS,
    )(own_x, factor_rows)


def forward_kernel(x_ref, piece0, piece1, piece2, piece3, rhs_ref, out_ref):
    own = x_ref[0]
    rhs = rhs_ref[...]
    for s, piece in enumerate((piece0, piece1, piece2, piece3)):
        product = jnp.dot(piece[...], rhs, preferred_element_type=F32).astype(BF16)
        out_ref[0, s ^ own] = product[:64]
        out_ref[1, s ^ own] = product[64:]


def forward_product(own_x, pieces, rhs):
    return pl.pallas_call(
        forward_kernel,
        out_shape=jax.ShapeDtypeStruct((2, 4, 64, RHS), BF16),
        in_specs=[SCALARS] + [VECTORS] * 5,
        out_specs=VECTORS,
    )(own_x, *pieces, rhs)


def backward_kernel(x_ref, piece0, piece1, piece2, piece3, vector_ref, out_ref):
    own = x_ref[0]
    total = jnp.zeros((1024, RHS), F32)
    for s, piece in enumerate((piece0, piece1, piece2, piece3)):
        vector = jnp.concatenate([vector_ref[0, s ^ own], vector_ref[1, s ^ own]], axis=0)
        total = total + lax.dot_general(
            piece[...], vector, (((0,), (0,)), ((), ())), preferred_element_type=F32
        )
    out_ref[...] = total.astype(BF16)


def backward_product(own_x, pieces, vector):
    return pl.pallas_call(
        backward_kernel,
        out_shape=jax.ShapeDtypeStruct((1024, RHS), BF16),
        in_specs=[SCALARS] + [VECTORS] * 5,
        out_specs=VECTORS,
    )(own_x, *pieces, vector)


def combine_kernel(tiles_ref, terms_ref, out_ref, total_ref):
    for p in range(LEAVES):
        for j in range(6):
            total_ref[6 * p + j] = -terms_ref[18 * p + 12 + j].astype(F32)
    for p in range(LEAVES):
        for k in range(LEAF_TILES):
            tile = tiles_ref[p, k]
            total_ref[tile] = total_ref[tile] + terms_ref[18 * p + k].astype(F32)
    out_ref[...] = (-total_ref[...]).astype(BF16)


def combine(root_tiles, terms):
    return pl.pallas_call(
        combine_kernel,
        out_shape=jax.ShapeDtypeStruct((ROOT_TILES, 8, RHS), BF16),
        in_specs=[
            pl.BlockSpec(memory_space=pltpu.SMEM),
            pl.BlockSpec(memory_space=pltpu.VMEM),
        ],
        out_specs=pl.BlockSpec(memory_space=pltpu.VMEM),
        scratch_shapes=[pltpu.VMEM((ROOT_TILES, 8, RHS), F32)],
    )(root_tiles, terms)


def granule_columns_kernel(source_ref, pivots_ref, out_ref):
    slot = lax.broadcasted_iota(jnp.int32, (8, TILE), 1) // 8
    tiles = [source_ref[:, t * TILE : (t + 1) * TILE].astype(F32) for t in range(ROOT_TILES)]
    for a in range(16):
        first = tiles[0] * 0.0
        second = pivots_ref[...]
        for t in range(16):
            first = jnp.where(slot == t, pltpu.roll(tiles[t], (t - a) * 8 % TILE, 1), first)
        for t in range(8):
            second = jnp.where(slot == t, pltpu.roll(tiles[16 + t], (t - a) * 8 % TILE, 1), second)
        out_ref[a, :, :TILE] = first.astype(BF16)
        out_ref[a, :, TILE:] = second.astype(BF16)


def granule_columns(rows, pivots):
    return pl.pallas_call(
        granule_columns_kernel,
        out_shape=jax.ShapeDtypeStruct((16, 8, 2 * TILE), BF16),
    )(rows, pivots)


def parts_of(value):
    high = lax.reduce_precision(value, 8, 7)
    rest = value - high
    middle = lax.reduce_precision(rest, 8, 7)
    low = lax.reduce_precision(rest - middle, 8, 7)
    return [high, middle, low]


def pivot_solve(values, diagonal, joined):
    length = values.shape[0]
    halves = values.reshape(length // 2, 2, values.shape[1])
    swapped = halves[:, ::-1, :].reshape(length, values.shape[1])
    return diagonal * values + joined * swapped


def other_core(value):
    return lax.ppermute(value, "c", [(0, 1), (1, 0)])


def both_cores(value):
    other = other_core(value)
    first = lax.axis_index("c") == 0
    return jnp.where(first, jnp.stack([value, other]), jnp.stack([other, value]))


def spread_granules(blocks):
    zl = lax.axis_index("zl")
    blocks = blocks.reshape((2, 2, 2, 2) + blocks.shape[1:])
    steps = (
        (3, "zh", 1, lax.axis_index("zh")),
        (1, "zl", 2, zl // 2),
        (2, "zl", 1, zl % 2),
        (0, "c", 1, lax.axis_index("c")),
    )
    for dim, axis, mask, bit in steps:
        low = bit == 0
        first = lax.index_in_dim(blocks, 0, dim, keepdims=False)
        second = lax.index_in_dim(blocks, 1, dim, keepdims=False)
        keep = jnp.where(low, first, second)
        send = jnp.where(low, second, first)
        other = lax.ppermute(send, axis, [(i, i ^ mask) for i in range(lax.axis_size(axis))])
        blocks = jnp.where(low, jnp.stack([keep, other], dim), jnp.stack([other, keep], dim))
    return blocks


def transposed_product(matrix, vector):
    return lax.dot_general(
        matrix, vector, (((0,), (0,)), ((), ())), preferred_element_type=F32
    )


def on_device(
    leaf_rhs,
    leaf_inverse,
    leaf_update,
    root_tiles,
    leaf_dinv,
    leaf_doff,
    leaf_pairs,
    root_rhs,
    root_inverse,
    root_dinv,
    root_doff,
    root_pairs,
):
    own_x = lax.axis_index("x").reshape(1)
    held = exchange(split_columns(own_x, leaf_inverse[0]), ("c",))
    pieces = [held[:, 0]]
    for s in range(1, 4):
        pieces.append(lax.ppermute(held[:, s], "x", [(i, i ^ s) for i in range(4)]))
    pieces = [piece.reshape(128, 1024) for piece in pieces]
    rhs_part = gather(leaf_rhs[0], YZ).reshape(1024, RHS)
    partial = forward_product(own_x, pieces, rhs_part).reshape(8, 64, RHS)
    leaf_forward = summed(exchange(partial, CX)).astype(BF16)

    joined = jnp.repeat(root_doff * root_pairs.astype(F32), 2)
    pivots = jnp.stack(parts_of(root_dinv) + parts_of(joined), axis=1)
    pivots = jnp.pad(pivots, ((0, 2), (64, TILE - 70)))
    root_block = granule_columns(jnp.pad(root_inverse, ((0, 2), (0, 0))), pivots)
    root_block = spread_granules(root_block).reshape(128, 2 * TILE)
    pivots = root_block[:, 192:198].astype(F32)
    dinv_rows = pivots[:, 0:1] + pivots[:, 1:2] + pivots[:, 2:3]
    joined_rows = pivots[:, 3:4] + pivots[:, 4:5] + pivots[:, 5:6]
    root_block = root_block[:, :192]

    update = leaf_update[0]
    ordered = update.reshape(12, 16, 8, 64).transpose(1, 0, 2, 3).reshape(16, 96, 64)
    at = jnp.arange(16 * 24, dtype=jnp.int32)
    row = TILE * (3 * lax.axis_index(YALL) + at // 8 % 3) + 8 * (at // 24) + at % 8
    row = row - 6 * lax.axis_index(AXES)
    select = (row[:, None] == jnp.arange(8, dtype=jnp.int32)[None, :]) & (row < 6)[:, None]
    select = select.astype(BF16).reshape(16, 24, 8)
    left = jnp.concatenate(
        [jnp.pad(ordered, ((0, 0), (0, 0), (0, 8))), jnp.pad(select, ((0, 0), (0, 0), (64, 0)))], 1
    ).reshape(1920, 72)
    right = jnp.concatenate([leaf_forward, jnp.pad(root_rhs, ((0, 2), (0, 0)))], 0)
    term = jnp.dot(left, right, preferred_element_type=F32).astype(BF16)
    term = summed(exchange(term.reshape(2, 960, RHS), ("c",))).astype(BF16)
    term = summed(exchange(term.reshape(8, 120, RHS), Z)).astype(BF16)
    term = summed(gather(term, ("x",))).astype(BF16)
    other = lax.ppermute(term, "yl", [(0, 1), (1, 0)])
    head = (term[:96].astype(F32) + other[:96].astype(F32)).astype(BF16)
    tail = jnp.where(
        lax.axis_index("yl") == 0,
        jnp.concatenate([term[96:], other[96:]], 0),
        jnp.concatenate([other[96:], term[96:]], 0),
    )
    term = gather(jnp.concatenate([head, tail], 0), ("p",)).reshape(72, 8, RHS)
    reduced = combine(root_tiles, term).reshape(192, RHS)

    forward = jnp.dot(root_block, reduced, preferred_element_type=F32)
    forward = forward + other_core(forward.astype(BF16)).astype(F32)
    forward = summed(gather(forward.astype(BF16), Z))
    root_scaled = pivot_solve(forward, dinv_rows, joined_rows).astype(BF16)
    back = transposed_product(root_block, root_scaled).astype(BF16)
    back = summed(exchange(back.reshape(4, 48, RHS), ("x",))).astype(BF16)
    root_part = summed(gather(back, YALL)).astype(BF16)
    root_full = both_cores(gather(root_part, ZX)).reshape(16, ROOT_TILES, 8, RHS)
    root_full = root_full.transpose(1, 0, 2, 3).reshape(ROOT_ROWS, RHS)
    root_own = lax.dynamic_slice_in_dim(root_full, lax.axis_index(AXES) * 6, 6, 0)

    tile_ids = lax.dynamic_index_in_dim(root_tiles, lax.axis_index("p"), 0, keepdims=False)
    onehot = (tile_ids[:, None] == jnp.arange(ROOT_TILES, dtype=jnp.int32)[None, :]).astype(BF16)
    tile_values = jnp.einsum(
        "kt,tar->kar", onehot, root_full.reshape(ROOT_TILES, TILE, RHS), preferred_element_type=F32
    )
    tile_values = tile_values.astype(BF16).reshape(LEAF_TILES * TILE, RHS)
    coupling = transposed_product(update, tile_values)
    leaf_joined = jnp.repeat(leaf_doff[0] * leaf_pairs[0].astype(F32), 2)[:, None]
    scaled = pivot_solve(leaf_forward.astype(F32), leaf_dinv[0][:, None], leaf_joined)
    leaf_vector = (scaled - coupling).astype(BF16)
    vector = gather(leaf_vector, CX).reshape(2, 4, 64, RHS)
    back_leaf = backward_product(own_x, pieces, vector)
    leaf_solution = summed(exchange(back_leaf.reshape(16, 64, RHS), YZ)).astype(BF16)
    return (leaf_solution[None], root_own)


def solution(mesh):
    fine = Mesh(mesh.devices.reshape(SIZES), AXES)
    in_specs = (
        P(LEAF, NODE, None),
        P(LEAF, NODE, None),
        P(LEAF, None, NODE),
        P(),
        P(LEAF, NODE),
        P(LEAF, NODE),
        P(LEAF, NODE),
        P(AXES, None),
        P(AXES, None),
        P(AXES),
        P(AXES),
        P(AXES),
    )
    out_specs = (P(LEAF, NODE, None), P(AXES, None))
    return jax.shard_map(
        on_device, mesh=fine, in_specs=in_specs, out_specs=out_specs, check_vma=False
    )
```

```python
import jax
import jax.numpy as jnp
from jax import lax
from jax.experimental import pallas as pl
from jax.experimental.pallas import tpu as pltpu
from jax.sharding import Mesh
from jax.sharding import PartitionSpec as P

LEAVES = 4
ROOT_TILES = 24
LEAF_TILES = 12
TILE = 128
RHS = 128
ROOT_ROWS = ROOT_TILES * TILE

AXES = ("p", "yl", "zl", "c", "zh", "x")
SIZES = (4, 2, 4, 2, 2, 4)
LEAF = ("p", "yl", "zl", "c")
NODE = ("zh", "x")
CX = ("c", "x")
YZ = ("yl", "zl", "zh")
YALL = ("p", "yl")
Z = ("zl", "zh")
ZX = ("zl", "zh", "x")

F32 = jnp.float32
BF16 = jnp.bfloat16


def exchange(blocks, axes):
    return lax.all_to_all(blocks, axes, 0, 0)


def gather(value, axes):
    count = 1
    for axis in axes:
        count *= lax.axis_size(axis)
    return exchange(jnp.broadcast_to(value[None], (count,) + value.shape), axes)


def summed(blocks):
    return jnp.sum(blocks.astype(F32), axis=0)


def split_columns_kernel(source_ref, out_ref):
    lane = lax.broadcasted_iota(jnp.int32, (64, TILE), 1)
    low = lane < 64
    for m in range(8):
        for core in range(2):
            for xh in range(2):
                first = ((m * 2 + core) * 2) * 2 + xh
                second = first + 2
                a = source_ref[:, first * TILE : (first + 1) * TILE].astype(F32)
                b = source_ref[:, second * TILE : (second + 1) * TILE].astype(F32)
                even = jnp.where(low, a, pltpu.roll(b, 64, 1))
                odd = jnp.where(low, pltpu.roll(a, 64, 1), b)
                place = slice(m * TILE, (m + 1) * TILE)
                out_ref[core * 4 + xh * 2, :, place] = even.astype(BF16)
                out_ref[core * 4 + xh * 2 + 1, :, place] = odd.astype(BF16)


def split_columns(factor_rows):
    return pl.pallas_call(
        split_columns_kernel,
        out_shape=jax.ShapeDtypeStruct((8, 64, 1024), BF16),
    )(factor_rows)


def combine_kernel(tiles_ref, terms_ref, out_ref, total_ref):
    for y in range(8):
        for j in range(3):
            total_ref[3 * y + j] = -terms_ref[15 * y + 12 + j].astype(F32)
    for p in range(LEAVES):
        for k in range(LEAF_TILES):
            tile = tiles_ref[p, k]
            term = terms_ref[30 * p + k].astype(F32) + terms_ref[30 * p + 15 + k].astype(F32)
            total_ref[tile] = total_ref[tile] + term
    out_ref[...] = (-total_ref[...]).astype(BF16)


def combine(root_tiles, terms):
    return pl.pallas_call(
        combine_kernel,
        out_shape=jax.ShapeDtypeStruct((ROOT_TILES, 8, RHS), BF16),
        in_specs=[
            pl.BlockSpec(memory_space=pltpu.SMEM),
            pl.BlockSpec(memory_space=pltpu.VMEM),
        ],
        out_specs=pl.BlockSpec(memory_space=pltpu.VMEM),
        scratch_shapes=[pltpu.VMEM((ROOT_TILES, 8, RHS), F32)],
    )(root_tiles, terms)


def granule_columns_kernel(source_ref, pivots_ref, out_ref):
    slot = lax.broadcasted_iota(jnp.int32, (8, TILE), 1) // 8
    tiles = [source_ref[:, t * TILE : (t + 1) * TILE].astype(F32) for t in range(ROOT_TILES)]
    for a in range(16):
        first = tiles[0] * 0.0
        second = pivots_ref[...]
        for t in range(16):
            first = jnp.where(slot == t, pltpu.roll(tiles[t], (t - a) * 8 % TILE, 1), first)
        for t in range(8):
            second = jnp.where(slot == t, pltpu.roll(tiles[16 + t], (t - a) * 8 % TILE, 1), second)
        out_ref[a, :, :TILE] = first.astype(BF16)
        out_ref[a, :, TILE:] = second.astype(BF16)


def granule_columns(rows, pivots):
    return pl.pallas_call(
        granule_columns_kernel,
        out_shape=jax.ShapeDtypeStruct((16, 8, 2 * TILE), BF16),
    )(rows, pivots)


def parts_of(value):
    high = lax.reduce_precision(value, 8, 7)
    rest = value - high
    middle = lax.reduce_precision(rest, 8, 7)
    low = lax.reduce_precision(rest - middle, 8, 7)
    return [high, middle, low]


def pivot_solve(values, diagonal, joined):
    length = values.shape[0]
    halves = values.reshape(length // 2, 2, values.shape[1])
    swapped = halves[:, ::-1, :].reshape(length, values.shape[1])
    return diagonal * values + joined * swapped


def other_core(value):
    return lax.ppermute(value, "c", [(0, 1), (1, 0)])


def both_cores(value):
    other = other_core(value)
    first = lax.axis_index("c") == 0
    return jnp.where(first, jnp.stack([value, other]), jnp.stack([other, value]))


def gather_leaf_rhs(value):
    def doubled(held, axis, mask, low, place):
        pairs = [(i, i ^ mask) for i in range(lax.axis_size(axis))]
        other = lax.ppermute(held, axis, pairs)
        return jnp.where(low, jnp.stack([held, other], place), jnp.stack([other, held], place))

    zl = lax.axis_index("zl")
    held = doubled(value, "zh", 1, lax.axis_index("zh") == 0, 0)
    held = doubled(held, "zl", 2, zl < 2, 0)
    held = doubled(held, "zl", 1, zl % 2 == 0, 1)
    held = doubled(held, "yl", 1, lax.axis_index("yl") == 0, 0)
    return held.reshape(1024, RHS)


def spread_granules(blocks):
    zl = lax.axis_index("zl")
    blocks = blocks.reshape((2, 2, 2, 2) + blocks.shape[1:])
    steps = (
        (3, "zh", 1, lax.axis_index("zh")),
        (1, "zl", 2, zl // 2),
        (2, "zl", 1, zl % 2),
        (0, "c", 1, lax.axis_index("c")),
    )
    for dim, axis, mask, bit in steps:
        low = bit == 0
        first = lax.index_in_dim(blocks, 0, dim, keepdims=False)
        second = lax.index_in_dim(blocks, 1, dim, keepdims=False)
        keep = jnp.where(low, first, second)
        send = jnp.where(low, second, first)
        other = lax.ppermute(send, axis, [(i, i ^ mask) for i in range(lax.axis_size(axis))])
        blocks = jnp.where(low, jnp.stack([keep, other], dim), jnp.stack([other, keep], dim))
    return blocks


def transposed_product(matrix, vector):
    return lax.dot_general(
        matrix, vector, (((0,), (0,)), ((), ())), preferred_element_type=F32
    )


def on_device(
    leaf_rhs,
    leaf_inverse,
    leaf_update,
    root_tiles,
    leaf_dinv,
    leaf_doff,
    leaf_pairs,
    root_rhs,
    root_inverse,
    root_dinv,
    root_doff,
    root_pairs,
):
    blocks = exchange(split_columns(leaf_inverse[0]), CX).reshape(512, 1024)
    rhs_part = gather_leaf_rhs(leaf_rhs[0])
    partial = jnp.dot(blocks, rhs_part, preferred_element_type=F32).astype(BF16)
    partial = exchange(partial.reshape(8, 64, RHS), CX)
    leaf_forward = summed(partial).astype(BF16)

    joined = jnp.repeat(root_doff * root_pairs.astype(F32), 2)
    pivots = jnp.stack(parts_of(root_dinv) + parts_of(joined), axis=1)
    pivots = jnp.pad(pivots, ((0, 2), (64, TILE - 70)))
    root_block = granule_columns(jnp.pad(root_inverse, ((0, 2), (0, 0))), pivots)
    root_block = spread_granules(root_block).reshape(128, 2 * TILE)
    pivots = root_block[:, 192:198].astype(F32)
    dinv_rows = pivots[:, 0:1] + pivots[:, 1:2] + pivots[:, 2:3]
    joined_rows = pivots[:, 3:4] + pivots[:, 4:5] + pivots[:, 5:6]
    root_block = root_block[:, :192]

    update = leaf_update[0]
    ordered = update.reshape(12, 16, 8, 64).transpose(1, 0, 2, 3).reshape(16, 96, 64)
    at = jnp.arange(16 * 24, dtype=jnp.int32)
    row = TILE * (3 * lax.axis_index(YALL) + at // 8 % 3) + 8 * (at // 24) + at % 8
    row = row - 6 * lax.axis_index(AXES)
    select = (row[:, None] == jnp.arange(8, dtype=jnp.int32)[None, :]) & (row < 6)[:, None]
    select = select.astype(BF16).reshape(16, 24, 8)
    left = jnp.concatenate(
        [jnp.pad(ordered, ((0, 0), (0, 0), (0, 8))), jnp.pad(select, ((0, 0), (0, 0), (64, 0)))], 1
    ).reshape(1920, 72)
    right = jnp.concatenate([leaf_forward, jnp.pad(root_rhs, ((0, 2), (0, 0)))], 0)
    term = jnp.dot(left, right, preferred_element_type=F32).astype(BF16)
    term = summed(exchange(term.reshape(2, 960, RHS), ("c",))).astype(BF16)
    term = exchange(term.reshape(8, 120, RHS), Z)
    term = summed(term).astype(BF16)
    term = gather(term, ("x",))
    term = summed(term).astype(BF16)
    term = gather(term, YALL)
    reduced = combine(root_tiles, term.reshape(120, 8, RHS)).reshape(192, RHS)

    forward = jnp.dot(root_block, reduced, preferred_element_type=F32)
    forward = forward + other_core(forward.astype(BF16)).astype(F32)
    forward = summed(gather(forward.astype(BF16), Z))
    root_scaled = pivot_solve(forward, dinv_rows, joined_rows).astype(BF16)
    back = transposed_product(root_block, root_scaled).astype(BF16)
    back = summed(exchange(back.reshape(4, 48, RHS), ("x",))).astype(BF16)
    root_part = summed(gather(back, YALL)).astype(BF16)
    root_full = both_cores(gather(root_part, ZX)).reshape(16, ROOT_TILES, 8, RHS)
    root_full = root_full.transpose(1, 0, 2, 3).reshape(ROOT_ROWS, RHS)
    root_own = lax.dynamic_slice_in_dim(root_full, lax.axis_index(AXES) * 6, 6, 0)

    tile_ids = lax.dynamic_index_in_dim(root_tiles, lax.axis_index("p"), 0, keepdims=False)
    onehot = (tile_ids[:, None] == jnp.arange(ROOT_TILES, dtype=jnp.int32)[None, :]).astype(BF16)
    tile_values = jnp.einsum(
        "kt,tar->kar", onehot, root_full.reshape(ROOT_TILES, TILE, RHS), preferred_element_type=F32
    )
    tile_values = tile_values.astype(BF16).reshape(LEAF_TILES * TILE, RHS)
    coupling = transposed_product(update, tile_values)
    leaf_joined = jnp.repeat(leaf_doff[0] * leaf_pairs[0].astype(F32), 2)[:, None]
    scaled = pivot_solve(leaf_forward.astype(F32), leaf_dinv[0][:, None], leaf_joined)
    leaf_vector = (scaled - coupling).astype(BF16)
    vector = gather(leaf_vector, CX).reshape(512, RHS)
    back_leaf = transposed_product(blocks, vector).astype(BF16)
    leaf_solution = summed(exchange(back_leaf.reshape(16, 64, RHS), YZ)).astype(BF16)
    return (leaf_solution[None], root_own)


def solution(mesh):
    fine = Mesh(mesh.devices.reshape(SIZES), AXES)
    in_specs = (
        P(LEAF, NODE, None),
        P(LEAF, NODE, None),
        P(LEAF, None, NODE),
        P(),
        P(LEAF, NODE),
        P(LEAF, NODE),
        P(LEAF, NODE),
        P(AXES, None),
        P(AXES, None),
        P(AXES),
        P(AXES),
        P(AXES),
    )
    out_specs = (P(LEAF, NODE, None), P(AXES, None))

    return jax.shard_map(
        on_device, mesh=fine, in_specs=in_specs, out_specs=out_specs, check_vma=False
    )
```

```python
import jax
import jax.numpy as jnp
from jax import lax
from jax.experimental import pallas as pl
from jax.experimental.pallas import tpu as pltpu
from jax.sharding import Mesh
from jax.sharding import PartitionSpec as P

LEAVES = 4
ROOT_TILES = 24
LEAF_TILES = 12
TILE = 128
RHS = 128
ROOT_ROWS = ROOT_TILES * TILE

AXES = ("p", "yl", "zl", "c", "zh", "x")
SIZES = (4, 2, 4, 2, 2, 4)
LEAF = ("p", "yl", "zl", "c")
NODE = ("zh", "x")
CX = ("c", "x")
YZ = ("yl", "zl", "zh")
YALL = ("p", "yl")
Z = ("zl", "zh")
ZX = ("zl", "zh", "x")

F32 = jnp.float32
BF16 = jnp.bfloat16


def exchange(blocks, axes):
    return lax.all_to_all(blocks, axes, 0, 0)


def gather(value, axes):
    count = 1
    for axis in axes:
        count *= lax.axis_size(axis)
    return exchange(jnp.broadcast_to(value[None], (count,) + value.shape), axes)


def summed(blocks):
    return jnp.sum(blocks.astype(F32), axis=0)


def split_columns_kernel(source_ref, out_ref):
    lane = lax.broadcasted_iota(jnp.int32, (64, TILE), 1)
    low = lane < 64
    for m in range(8):
        for core in range(2):
            for xh in range(2):
                first = ((m * 2 + core) * 2) * 2 + xh
                second = first + 2
                a = source_ref[:, first * TILE : (first + 1) * TILE].astype(F32)
                b = source_ref[:, second * TILE : (second + 1) * TILE].astype(F32)
                even = jnp.where(low, a, pltpu.roll(b, 64, 1))
                odd = jnp.where(low, pltpu.roll(a, 64, 1), b)
                place = slice(m * TILE, (m + 1) * TILE)
                out_ref[core * 4 + xh * 2, :, place] = even.astype(BF16)
                out_ref[core * 4 + xh * 2 + 1, :, place] = odd.astype(BF16)


def split_columns(factor_rows):
    return pl.pallas_call(
        split_columns_kernel,
        out_shape=jax.ShapeDtypeStruct((8, 64, 1024), BF16),
    )(factor_rows)


def combine_kernel(tiles_ref, terms_ref, out_ref, total_ref):
    for y in range(8):
        for j in range(3):
            total_ref[3 * y + j] = -terms_ref[15 * y + 12 + j].astype(F32)
    for p in range(LEAVES):
        for k in range(LEAF_TILES):
            tile = tiles_ref[p, k]
            term = terms_ref[30 * p + k].astype(F32) + terms_ref[30 * p + 15 + k].astype(F32)
            total_ref[tile] = total_ref[tile] + term
    out_ref[...] = (-total_ref[...]).astype(BF16)


def combine(root_tiles, terms):
    return pl.pallas_call(
        combine_kernel,
        out_shape=jax.ShapeDtypeStruct((ROOT_TILES, 8, RHS), BF16),
        in_specs=[
            pl.BlockSpec(memory_space=pltpu.SMEM),
            pl.BlockSpec(memory_space=pltpu.VMEM),
        ],
        out_specs=pl.BlockSpec(memory_space=pltpu.VMEM),
        scratch_shapes=[pltpu.VMEM((ROOT_TILES, 8, RHS), F32)],
    )(root_tiles, terms)


def granule_columns_kernel(source_ref, pivots_ref, out_ref):
    lane = lax.broadcasted_iota(jnp.int32, (6, TILE), 1)
    slot = lane // 8
    tiles = [source_ref[:, t * TILE : (t + 1) * TILE].astype(F32) for t in range(ROOT_TILES)]
    spare = jnp.zeros((6, TILE), F32)
    for j in range(6):
        spare = jnp.where(lane == 64 + j, pivots_ref[:, j : j + 1], spare)
    out_ref[...] = jnp.zeros_like(out_ref)
    for a in range(16):
        first = spare
        second = spare
        for t in range(16):
            first = jnp.where(slot == t, pltpu.roll(tiles[t], (t - a) * 8 % TILE, 1), first)
        for t in range(8):
            second = jnp.where(slot == t, pltpu.roll(tiles[16 + t], (t - a) * 8 % TILE, 1), second)
        out_ref[a, 0, :6] = first.astype(BF16)
        out_ref[a, 1, :6] = second.astype(BF16)


def granule_columns(rows, pivots):
    return pl.pallas_call(
        granule_columns_kernel,
        out_shape=jax.ShapeDtypeStruct((16, 2, 8, TILE), BF16),
    )(rows, pivots)


def parts_of(value):
    high = lax.reduce_precision(value, 8, 7)
    rest = value - high
    middle = lax.reduce_precision(rest, 8, 7)
    low = lax.reduce_precision(rest - middle, 8, 7)
    return [high, middle, low]


def pivot_solve(values, diagonal, joined):
    length = values.shape[0]
    halves = values.reshape(length // 2, 2, values.shape[1])
    swapped = halves[:, ::-1, :].reshape(length, values.shape[1])
    return diagonal * values + joined * swapped


def other_core(value):
    return lax.ppermute(value, "c", [(0, 1), (1, 0)])


def both_cores(value):
    other = other_core(value)
    first = lax.axis_index("c") == 0
    return jnp.where(first, jnp.stack([value, other]), jnp.stack([other, value]))


def gather_leaf_rhs(value):
    def doubled(held, axis, mask, low, place):
        pairs = [(i, i ^ mask) for i in range(lax.axis_size(axis))]
        other = lax.ppermute(held, axis, pairs)
        return jnp.where(low, jnp.stack([held, other], place), jnp.stack([other, held], place))

    zl = lax.axis_index("zl")
    held = doubled(value, "zh", 1, lax.axis_index("zh") == 0, 0)
    held = doubled(held, "zl", 2, zl < 2, 0)
    held = doubled(held, "zl", 1, zl % 2 == 0, 1)
    held = doubled(held, "yl", 1, lax.axis_index("yl") == 0, 0)
    return held.reshape(1024, RHS)


def transposed_product(matrix, vector):
    return lax.dot_general(
        matrix, vector, (((0,), (0,)), ((), ())), preferred_element_type=F32
    )


def on_device(
    leaf_rhs,
    leaf_inverse,
    leaf_update,
    root_tiles,
    leaf_dinv,
    leaf_doff,
    leaf_pairs,
    root_rhs,
    root_inverse,
    root_dinv,
    root_doff,
    root_pairs,
):
    blocks = exchange(split_columns(leaf_inverse[0]), CX).reshape(512, 1024)
    rhs_part = gather_leaf_rhs(leaf_rhs[0])
    partial = jnp.dot(blocks, rhs_part, preferred_element_type=F32).astype(BF16)
    partial = exchange(partial.reshape(8, 64, RHS), CX)
    leaf_forward = summed(partial).astype(BF16)

    joined = jnp.repeat(root_doff * root_pairs.astype(F32), 2)
    pivots = jnp.stack(parts_of(root_dinv) + parts_of(joined), axis=1)
    root_block = granule_columns(root_inverse, pivots)

    update = leaf_update[0]
    ordered = update.reshape(12, 16, 8, 64).transpose(1, 0, 2, 3).reshape(16, 96, 64)
    at = jnp.arange(16 * 24, dtype=jnp.int32)
    row = TILE * (3 * lax.axis_index(YALL) + at // 8 % 3) + 8 * (at // 24) + at % 8
    row = row - 6 * lax.axis_index(AXES)
    select = (row[:, None] == jnp.arange(8, dtype=jnp.int32)[None, :]) & (row < 6)[:, None]
    select = select.astype(BF16).reshape(16, 24, 8)
    left = jnp.concatenate(
        [jnp.pad(ordered, ((0, 0), (0, 0), (0, 8))), jnp.pad(select, ((0, 0), (0, 0), (64, 0)))], 1
    ).reshape(1920, 72)
    right = jnp.concatenate([leaf_forward, jnp.pad(root_rhs, ((0, 2), (0, 0)))], 0)
    term = jnp.dot(left, right, preferred_element_type=F32).astype(BF16)
    term = jnp.concatenate([term.reshape(2, 8, 120, RHS), root_block.reshape(2, 8, 16, RHS)], 2)
    term = exchange(term.reshape(2, 1088, RHS), ("c",)).reshape(2, 8, 136, RHS)
    root_block = term[:, :, 120:].transpose(1, 0, 2, 3).reshape(8, 32, RHS)
    term = summed(term[:, :, :120]).astype(BF16)
    term = exchange(jnp.concatenate([term, root_block], 1), Z)
    root_block = term[:, 120:].reshape(8, 2, 2, 8, RHS).transpose(0, 1, 3, 2, 4).reshape(128, 2 * TILE)
    pivots = root_block[:, 192:198].astype(F32)
    dinv_rows = pivots[:, 0:1] + pivots[:, 1:2] + pivots[:, 2:3]
    joined_rows = pivots[:, 3:4] + pivots[:, 4:5] + pivots[:, 5:6]
    root_block = root_block[:, :192]
    term = summed(term[:, :120]).astype(BF16)
    term = summed(gather(term, ("x",))).astype(BF16)
    reduced = combine(root_tiles, gather(term, YALL).reshape(120, 8, RHS)).reshape(192, RHS)

    forward = jnp.dot(root_block, reduced, preferred_element_type=F32)
    forward = forward + other_core(forward.astype(BF16)).astype(F32)
    forward = summed(gather(forward.astype(BF16), Z))
    root_scaled = pivot_solve(forward, dinv_rows, joined_rows).astype(BF16)
    back = transposed_product(root_block, root_scaled).astype(BF16)
    back = summed(exchange(back.reshape(4, 48, RHS), ("x",))).astype(BF16)
    root_part = summed(gather(back, YALL)).astype(BF16)
    root_full = both_cores(gather(root_part, ZX)).reshape(16, ROOT_TILES, 8, RHS)
    root_full = root_full.transpose(1, 0, 2, 3).reshape(ROOT_ROWS, RHS)
    root_own = lax.dynamic_slice_in_dim(root_full, lax.axis_index(AXES) * 6, 6, 0)

    tile_ids = lax.dynamic_index_in_dim(root_tiles, lax.axis_index("p"), 0, keepdims=False)
    onehot = (tile_ids[:, None] == jnp.arange(ROOT_TILES, dtype=jnp.int32)[None, :]).astype(BF16)
    tile_values = jnp.einsum(
        "kt,tar->kar", onehot, root_full.reshape(ROOT_TILES, TILE, RHS), preferred_element_type=F32
    )
    tile_values = tile_values.astype(BF16).reshape(LEAF_TILES * TILE, RHS)
    coupling = transposed_product(update, tile_values)
    leaf_joined = jnp.repeat(leaf_doff[0] * leaf_pairs[0].astype(F32), 2)[:, None]
    scaled = pivot_solve(leaf_forward.astype(F32), leaf_dinv[0][:, None], leaf_joined)
    leaf_vector = (scaled - coupling).astype(BF16)
    vector = gather(leaf_vector, CX).reshape(512, RHS)
    back_leaf = transposed_product(blocks, vector).astype(BF16)
    leaf_solution = summed(exchange(back_leaf.reshape(16, 64, RHS), YZ)).astype(BF16)
    return (leaf_solution[None], root_own)


def solution(mesh):
    fine = Mesh(mesh.devices.reshape(SIZES), AXES)
    in_specs = (
        P(LEAF, NODE, None),
        P(LEAF, NODE, None),
        P(LEAF, None, NODE),
        P(),
        P(LEAF, NODE),
        P(LEAF, NODE),
        P(LEAF, NODE),
        P(AXES, None),
        P(AXES, None),
        P(AXES),
        P(AXES),
        P(AXES),
    )
    out_specs = (P(LEAF, NODE, None), P(AXES, None))

    return jax.shard_map(
        on_device, mesh=fine, in_specs=in_specs, out_specs=out_specs, check_vma=False
    )
```

```python
import jax
import jax.numpy as jnp
from jax import lax
from jax.experimental import pallas as pl
from jax.experimental.pallas import tpu as pltpu
from jax.sharding import Mesh
from jax.sharding import PartitionSpec as P

LEAVES = 4
ROOT_TILES = 24
LEAF_TILES = 12
TILE = 128
RHS = 128
ROOT_ROWS = ROOT_TILES * TILE

AXES = ("p", "yl", "zl", "c", "zh", "x")
SIZES = (4, 2, 4, 2, 2, 4)
LEAF = ("p", "yl", "zl", "c")
NODE = ("zh", "x")
CX = ("c", "x")
YZ = ("yl", "zl", "zh")
YALL = ("p", "yl")
Z = ("zl", "zh")
ZX = ("zl", "zh", "x")

F32 = jnp.float32
BF16 = jnp.bfloat16


def exchange(blocks, axes):
    return lax.all_to_all(blocks, axes, 0, 0)


def gather(value, axes):
    count = 1
    for axis in axes:
        count *= lax.axis_size(axis)
    return exchange(jnp.broadcast_to(value[None], (count,) + value.shape), axes)


def summed(blocks):
    return jnp.sum(blocks.astype(F32), axis=0)


SCALARS = pl.BlockSpec(memory_space=pltpu.SMEM)
VECTORS = pl.BlockSpec(memory_space=pltpu.VMEM)


def split_columns_kernel(source_ref, out_ref):
    lane = lax.broadcasted_iota(jnp.int32, (64, TILE), 1)
    low = lane < 64
    for m in range(8):
        for core in range(2):
            for xh in range(2):
                first = ((m * 2 + core) * 2) * 2 + xh
                second = first + 2
                a = source_ref[:, first * TILE : (first + 1) * TILE].astype(F32)
                b = source_ref[:, second * TILE : (second + 1) * TILE].astype(F32)
                even = jnp.where(low, a, pltpu.roll(b, 64, 1))
                odd = jnp.where(low, pltpu.roll(a, 64, 1), b)
                place = slice(m * TILE, (m + 1) * TILE)
                out_ref[core * 4 + xh * 2, :, place] = even.astype(BF16)
                out_ref[core * 4 + xh * 2 + 1, :, place] = odd.astype(BF16)


def split_columns(factor_rows):
    return pl.pallas_call(
        split_columns_kernel,
        out_shape=jax.ShapeDtypeStruct((8, 64, 1024), BF16),
    )(factor_rows)


def combine_kernel(tiles_ref, terms_ref, block_ref, wide_ref, narrow_ref, total_ref):
    for y in range(8):
        for j in range(3):
            total_ref[3 * y + j] = -terms_ref[15 * y + 12 + j].astype(F32)
        total_ref[ROOT_TILES + y] = jnp.zeros((8, RHS), F32)
    for p in range(LEAVES):
        for k in range(LEAF_TILES):
            tile = tiles_ref[p, k]
            term = terms_ref[30 * p + k].astype(F32) + terms_ref[30 * p + 15 + k].astype(F32)
            total_ref[tile] = total_ref[tile] + term
    reduced = (-total_ref[...]).reshape(256, RHS).astype(BF16)
    product = jnp.dot(block_ref[...], reduced, preferred_element_type=F32)
    wide_ref[...] = product
    narrow_ref[...] = product.astype(BF16)


def combine(root_tiles, terms, block):
    return pl.pallas_call(
        combine_kernel,
        out_shape=(
            jax.ShapeDtypeStruct((TILE, RHS), F32),
            jax.ShapeDtypeStruct((TILE, RHS), BF16),
        ),
        in_specs=[SCALARS, VECTORS, VECTORS],
        out_specs=(VECTORS, VECTORS),
        scratch_shapes=[pltpu.VMEM((ROOT_TILES + 8, 8, RHS), F32)],
    )(root_tiles, terms, block)


def granule_columns_kernel(dinv_ref, doff_ref, pairs_ref, source_ref, out_ref):
    lane = lax.broadcasted_iota(jnp.int32, (6, TILE), 1)
    slot = lane // 8
    tiles = [source_ref[:, t * TILE : (t + 1) * TILE].astype(F32) for t in range(ROOT_TILES)]
    row = lax.broadcasted_iota(jnp.int32, (6, TILE), 0)
    diagonal = jnp.zeros((6, TILE), F32)
    joined = jnp.zeros((6, TILE), F32)
    for i in range(6):
        diagonal = jnp.where(row == i, dinv_ref[i], diagonal)
        both = doff_ref[i // 2] * pairs_ref[i // 2].astype(F32)
        joined = jnp.where(row == i, both, joined)
    spare = jnp.zeros((6, TILE), F32)
    for j, part in enumerate(parts_of(diagonal) + parts_of(joined)):
        spare = jnp.where(lane == 64 + j, part, spare)
    out_ref[...] = jnp.zeros_like(out_ref)
    for a in range(16):
        first = spare
        second = spare
        for t in range(16):
            first = jnp.where(slot == t, pltpu.roll(tiles[t], (t - a) * 8 % TILE, 1), first)
        for t in range(8):
            second = jnp.where(slot == t, pltpu.roll(tiles[16 + t], (t - a) * 8 % TILE, 1), second)
        out_ref[a, 0, :6] = first.astype(BF16)
        out_ref[a, 1, :6] = second.astype(BF16)


def granule_columns(dinv, doff, pairs, rows):
    return pl.pallas_call(
        granule_columns_kernel,
        out_shape=jax.ShapeDtypeStruct((16, 2, 8, TILE), BF16),
        in_specs=[SCALARS, SCALARS, SCALARS, VECTORS],
        out_specs=VECTORS,
    )(dinv, doff, pairs, rows)


def parts_of(value):
    high = value.astype(BF16).astype(F32)
    rest = value - high
    middle = rest.astype(BF16).astype(F32)
    low = (rest - middle).astype(BF16).astype(F32)
    return [high, middle, low]


def pivot_solve(values, diagonal, joined):
    length = values.shape[0]
    halves = values.reshape(length // 2, 2, values.shape[1])
    swapped = halves[:, ::-1, :].reshape(length, values.shape[1])
    return diagonal * values + joined * swapped


def other_core(value):
    return lax.ppermute(value, "c", [(0, 1), (1, 0)])


def both_cores(value):
    other = other_core(value)
    first = lax.axis_index("c") == 0
    return jnp.where(first, jnp.stack([value, other]), jnp.stack([other, value]))


def gather_leaf_rhs(value):
    def doubled(held, axis, mask, low, place):
        pairs = [(i, i ^ mask) for i in range(lax.axis_size(axis))]
        other = lax.ppermute(held, axis, pairs)
        return jnp.where(low, jnp.stack([held, other], place), jnp.stack([other, held], place))

    zl = lax.axis_index("zl")
    held = doubled(value, "zh", 1, lax.axis_index("zh") == 0, 0)
    held = doubled(held, "zl", 2, zl < 2, 0)
    held = doubled(held, "zl", 1, zl % 2 == 0, 1)
    held = doubled(held, "yl", 1, lax.axis_index("yl") == 0, 0)
    return held.reshape(1024, RHS)


def transposed_product(matrix, vector):
    return lax.dot_general(
        matrix, vector, (((0,), (0,)), ((), ())), preferred_element_type=F32
    )


def on_device(
    leaf_rhs,
    leaf_inverse,
    leaf_update,
    root_tiles,
    leaf_dinv,
    leaf_doff,
    leaf_pairs,
    root_rhs,
    root_inverse,
    root_dinv,
    root_doff,
    root_pairs,
):
    blocks = exchange(split_columns(leaf_inverse[0]), CX).reshape(512, 1024)
    rhs_part = gather_leaf_rhs(leaf_rhs[0])
    partial = jnp.dot(blocks, rhs_part, preferred_element_type=F32).astype(BF16)
    update = leaf_update[0]
    at = jnp.arange(16 * 24, dtype=jnp.int32)
    partial, late_update, at = lax.optimization_barrier((partial, update, at))
    partial = exchange(partial.reshape(8, 64, RHS), CX)
    leaf_forward = summed(partial).astype(BF16)

    root_block = granule_columns(root_dinv, root_doff, root_pairs, root_inverse)

    ordered = late_update.reshape(12, 16, 8, 64).transpose(1, 0, 2, 3).reshape(16, 96, 64)
    row = TILE * (3 * lax.axis_index(YALL) + at // 8 % 3) + 8 * (at // 24) + at % 8
    row = row - 6 * lax.axis_index(AXES)
    select = (row[:, None] == jnp.arange(8, dtype=jnp.int32)[None, :]) & (row < 6)[:, None]
    select = select.astype(BF16).reshape(16, 24, 8)
    left = jnp.concatenate(
        [jnp.pad(ordered, ((0, 0), (0, 0), (0, 8))), jnp.pad(select, ((0, 0), (0, 0), (64, 0)))], 1
    ).reshape(1920, 72)
    right = jnp.concatenate([leaf_forward, jnp.pad(root_rhs, ((0, 2), (0, 0)))], 0)
    term = jnp.dot(left, right, preferred_element_type=F32).astype(BF16)
    term = jnp.concatenate([term.reshape(2, 8, 120, RHS), root_block.reshape(2, 8, 16, RHS)], 2)
    term = exchange(term.reshape(2, 1088, RHS), ("c",)).reshape(2, 8, 136, RHS)
    root_block = term[:, :, 120:].transpose(1, 0, 2, 3).reshape(8, 32, RHS)
    term = summed(term[:, :, :120]).astype(BF16)
    term = exchange(jnp.concatenate([term, root_block], 1), Z)
    root_block = term[:, 120:].reshape(8, 2, 2, 8, RHS).transpose(0, 1, 3, 2, 4).reshape(128, 2 * TILE)
    pivots = root_block[:, 192:198].astype(F32)
    dinv_rows = pivots[:, 0:1] + pivots[:, 1:2] + pivots[:, 2:3]
    joined_rows = pivots[:, 3:4] + pivots[:, 4:5] + pivots[:, 5:6]
    term = summed(term[:, :120]).astype(BF16)
    term = summed(gather(term, ("x",))).astype(BF16)
    term = gather(term, YALL).reshape(120, 8, RHS)

    wide, narrow = combine(root_tiles, term, root_block)
    forward = wide + other_core(narrow).astype(F32)
    forward = summed(gather(forward.astype(BF16), Z))
    root_scaled = pivot_solve(forward, dinv_rows, joined_rows).astype(BF16)
    back = transposed_product(root_block[:, :192], root_scaled).astype(BF16)
    back = summed(exchange(back.reshape(4, 48, RHS), ("x",))).astype(BF16)
    root_part = summed(gather(back, YALL)).astype(BF16)
    root_full = both_cores(gather(root_part, ZX)).reshape(16, ROOT_TILES, 8, RHS)
    root_full = root_full.transpose(1, 0, 2, 3).reshape(ROOT_ROWS, RHS)
    root_own = lax.dynamic_slice_in_dim(root_full, lax.axis_index(AXES) * 6, 6, 0)

    tile_ids = lax.dynamic_index_in_dim(root_tiles, lax.axis_index("p"), 0, keepdims=False)
    onehot = (tile_ids[:, None] == jnp.arange(ROOT_TILES, dtype=jnp.int32)[None, :]).astype(BF16)
    tile_values = jnp.einsum(
        "kt,tar->kar", onehot, root_full.reshape(ROOT_TILES, TILE, RHS), preferred_element_type=F32
    )
    tile_values = tile_values.astype(BF16).reshape(LEAF_TILES * TILE, RHS)
    coupling = transposed_product(update, tile_values)
    leaf_joined = jnp.repeat(leaf_doff[0] * leaf_pairs[0].astype(F32), 2)[:, None]
    scaled = pivot_solve(leaf_forward.astype(F32), leaf_dinv[0][:, None], leaf_joined)
    leaf_vector = (scaled - coupling).astype(BF16)
    vector = gather(leaf_vector, CX).reshape(512, RHS)
    back_leaf = transposed_product(blocks, vector).astype(BF16)
    leaf_solution = summed(exchange(back_leaf.reshape(16, 64, RHS), YZ)).astype(BF16)
    return (leaf_solution[None], root_own)


def solution(mesh):
    fine = Mesh(mesh.devices.reshape(SIZES), AXES)
    in_specs = (
        P(LEAF, NODE, None),
        P(LEAF, NODE, None),
        P(LEAF, None, NODE),
        P(),
        P(LEAF, NODE),
        P(LEAF, NODE),
        P(LEAF, NODE),
        P(AXES, None),
        P(AXES, None),
        P(AXES),
        P(AXES),
        P(AXES),
    )
    out_specs = (P(LEAF, NODE, None), P(AXES, None))

    return jax.shard_map(
        on_device, mesh=fine, in_specs=in_specs, out_specs=out_specs, check_vma=False
    )
```

```python
import jax
import jax.numpy as jnp
from jax import lax
from jax.experimental import pallas as pl
from jax.experimental.pallas import tpu as pltpu
from jax.experimental.layout import Layout, with_layout_constraint
from jax.sharding import Mesh
from jax.sharding import PartitionSpec as P

LEAVES = 4
ROOT_TILES = 24
LEAF_TILES = 12
TILE = 128
RHS = 128
ROOT_ROWS = ROOT_TILES * TILE

AXES = ("p", "yl", "zl", "c", "zh", "x")
SIZES = (4, 2, 4, 2, 2, 4)
LEAF = ("p", "yl", "zl", "c")
NODE = ("zh", "x")
CX = ("c", "x")
YZ = ("yl", "zl", "zh")
YALL = ("p", "yl")
Z = ("zl", "zh")
ZX = ("zl", "zh", "x")

F32 = jnp.float32
BF16 = jnp.bfloat16


def exchange(blocks, axes):
    return lax.all_to_all(blocks, axes, 0, 0)


def gather(value, axes):
    count = 1
    for axis in axes:
        count *= lax.axis_size(axis)
    return exchange(jnp.broadcast_to(value[None], (count,) + value.shape), axes)


def summed(blocks):
    return jnp.sum(blocks.astype(F32), axis=0)


SCALARS = pl.BlockSpec(memory_space=pltpu.SMEM)
VECTORS = pl.BlockSpec(memory_space=pltpu.VMEM)


def split_columns_kernel(source_ref, out_ref):
    lane = lax.broadcasted_iota(jnp.int32, (64, TILE), 1)
    low = lane < 64
    for m in range(8):
        for core in range(2):
            for xh in range(2):
                first = ((m * 2 + core) * 2) * 2 + xh
                second = first + 2
                a = source_ref[:, first * TILE : (first + 1) * TILE].astype(F32)
                b = source_ref[:, second * TILE : (second + 1) * TILE].astype(F32)
                even = jnp.where(low, a, pltpu.roll(b, 64, 1))
                odd = jnp.where(low, pltpu.roll(a, 64, 1), b)
                place = slice(m * TILE, (m + 1) * TILE)
                out_ref[core * 4 + xh * 2, :, place] = even.astype(BF16)
                out_ref[core * 4 + xh * 2 + 1, :, place] = odd.astype(BF16)


def split_columns(factor_rows):
    return pl.pallas_call(
        split_columns_kernel,
        out_shape=jax.ShapeDtypeStruct((8, 64, 1024), BF16),
    )(factor_rows)


def combine_kernel(tiles_ref, terms_ref, block_ref, out_ref, total_ref):
    for y in range(8):
        for x in range(3):
            total_ref[3 * y + x] = -terms_ref[(x * 8 + y) * 4 + 3].astype(F32)
        total_ref[ROOT_TILES + y] = jnp.zeros((8, RHS), F32)
    for p in range(LEAVES):
        for x in range(4):
            for k in range(3):
                tile = tiles_ref[p, 3 * x + k]
                first = (x * 8 + 2 * p) * 4 + k
                term = terms_ref[first].astype(F32) + terms_ref[first + 4].astype(F32)
                total_ref[tile] = total_ref[tile] + term
    reduced = (-total_ref[...]).reshape(256, RHS).astype(BF16)
    product = jnp.dot(block_ref[...], reduced, preferred_element_type=F32)
    out_ref[...] = product.astype(BF16)


def combine(root_tiles, terms, block):
    return pl.pallas_call(
        combine_kernel,
        out_shape=jax.ShapeDtypeStruct((TILE, RHS), BF16),
        in_specs=[SCALARS, VECTORS, VECTORS],
        out_specs=VECTORS,
        scratch_shapes=[pltpu.VMEM((ROOT_TILES + 8, 8, RHS), F32)],
    )(root_tiles, terms, block)


def granule_columns_kernel(dinv_ref, doff_ref, pairs_ref, source_ref, out_ref):
    lane = lax.broadcasted_iota(jnp.int32, (6, TILE), 1)
    slot = lane // 8
    tiles = [source_ref[:, t * TILE : (t + 1) * TILE].astype(F32) for t in range(ROOT_TILES)]
    row = lax.broadcasted_iota(jnp.int32, (6, TILE), 0)
    diagonal = jnp.zeros((6, TILE), F32)
    joined = jnp.zeros((6, TILE), F32)
    for i in range(6):
        diagonal = jnp.where(row == i, dinv_ref[i], diagonal)
        both = doff_ref[i // 2] * pairs_ref[i // 2].astype(F32)
        joined = jnp.where(row == i, both, joined)
    spare = jnp.zeros((6, TILE), F32)
    for j, part in enumerate(parts_of(diagonal) + parts_of(joined)):
        spare = jnp.where(lane == 64 + j, part, spare)
    out_ref[...] = jnp.zeros_like(out_ref)
    for a in range(16):
        first = spare
        second = spare
        for t in range(16):
            first = jnp.where(slot == t, pltpu.roll(tiles[t], (t - a) * 8 % TILE, 1), first)
        for t in range(8):
            second = jnp.where(slot == t, pltpu.roll(tiles[16 + t], (t - a) * 8 % TILE, 1), second)
        out_ref[a, 0, :6] = first.astype(BF16)
        out_ref[a, 1, :6] = second.astype(BF16)


def granule_columns(dinv, doff, pairs, rows):
    return pl.pallas_call(
        granule_columns_kernel,
        out_shape=jax.ShapeDtypeStruct((16, 2, 8, TILE), BF16),
        in_specs=[SCALARS, SCALARS, SCALARS, VECTORS],
        out_specs=VECTORS,
    )(dinv, doff, pairs, rows)


def parts_of(value):
    high = value.astype(BF16).astype(F32)
    rest = value - high
    middle = rest.astype(BF16).astype(F32)
    low = (rest - middle).astype(BF16).astype(F32)
    return [high, middle, low]


def pivot_solve(values, diagonal, joined):
    length = values.shape[0]
    halves = values.reshape(length // 2, 2, values.shape[1])
    swapped = halves[:, ::-1, :].reshape(length, values.shape[1])
    return diagonal * values + joined * swapped


def other_core(value):
    return lax.ppermute(value, "c", [(0, 1), (1, 0)])


def both_cores(value):
    other = other_core(value)
    first = lax.axis_index("c") == 0
    return jnp.where(first, jnp.stack([value, other]), jnp.stack([other, value]))


def gather_leaf_rhs(value):
    def doubled(held, axis, mask, low, place):
        pairs = [(i, i ^ mask) for i in range(lax.axis_size(axis))]
        other = lax.ppermute(held, axis, pairs)
        return jnp.where(low, jnp.stack([held, other], place), jnp.stack([other, held], place))

    zl = lax.axis_index("zl")
    held = doubled(value, "zh", 1, lax.axis_index("zh") == 0, 0)
    held = doubled(held, "zl", 2, zl < 2, 0)
    held = doubled(held, "zl", 1, zl % 2 == 0, 1)
    held = doubled(held, "yl", 1, lax.axis_index("yl") == 0, 0)
    return held.reshape(1024, RHS)


def transposed_product(matrix, vector):
    return lax.dot_general(
        matrix, vector, (((0,), (0,)), ((), ())), preferred_element_type=F32
    )


def on_device(
    leaf_rhs,
    leaf_inverse,
    leaf_update,
    root_tiles,
    leaf_dinv,
    leaf_doff,
    leaf_pairs,
    root_rhs,
    root_inverse,
    root_dinv,
    root_doff,
    root_pairs,
):
    blocks = exchange(split_columns(leaf_inverse[0]), CX).reshape(512, 1024)
    rhs_part = gather_leaf_rhs(leaf_rhs[0])
    partial = jnp.dot(blocks, rhs_part, preferred_element_type=F32)
    partial = with_layout_constraint(partial, Layout(major_to_minor=(0, 1))).astype(BF16)
    update = leaf_update[0]
    at = jnp.arange(512, dtype=jnp.int32)
    partial, late_update, at = lax.optimization_barrier((partial, update, at))
    partial = exchange(partial.reshape(8, 64, RHS), CX)
    leaf_forward = summed(partial).astype(BF16)

    root_block = granule_columns(root_dinv, root_doff, root_pairs, root_inverse)

    ordered = late_update.reshape(4, 3, 2, 8, 8, 64).transpose(2, 0, 3, 1, 4, 5)
    ordered = ordered.reshape(64, 24, 64)
    x_of = at // 64 % 4
    row = TILE * (3 * lax.axis_index(YALL) + x_of) + 8 * (at // 256 * 8 + at // 8 % 8) + at % 8
    row = jnp.where(x_of < 3, row, -1) - 6 * lax.axis_index(AXES)
    select = (row[:, None] == jnp.arange(8, dtype=jnp.int32)[None, :]) & (row < 6)[:, None]
    select = select.astype(BF16).reshape(64, 8, 8)
    left = jnp.concatenate(
        [jnp.pad(ordered, ((0, 0), (0, 0), (0, 8))), jnp.pad(select, ((0, 0), (0, 0), (64, 0)))], 1
    ).reshape(2048, 72)
    right = jnp.concatenate([leaf_forward, jnp.pad(root_rhs, ((0, 2), (0, 0)))], 0)
    term = jnp.dot(left, right, preferred_element_type=F32).astype(BF16)
    term = jnp.concatenate([term.reshape(2, 1024, RHS), root_block.reshape(2, 128, RHS)], 1)
    term = exchange(term, ("c",))
    root_block = term[:, 1024:].reshape(2, 8, 16, RHS).transpose(1, 0, 2, 3).reshape(8, 32, RHS)
    term = summed(term[:, :1024]).astype(BF16)
    term = summed(exchange(term.reshape(4, 256, RHS), ("x",))).astype(BF16)
    term = exchange(jnp.concatenate([term.reshape(8, 32, RHS), root_block], 1), Z)
    root_block = term[:, 32:].reshape(8, 2, 2, 8, RHS).transpose(0, 1, 3, 2, 4).reshape(128, 2 * TILE)
    pivots = root_block[:, 192:198].astype(F32)
    dinv_rows = pivots[:, 0:1] + pivots[:, 1:2] + pivots[:, 2:3]
    joined_rows = pivots[:, 3:4] + pivots[:, 4:5] + pivots[:, 5:6]
    term = summed(term[:, :32]).astype(BF16)
    term = gather(gather(term, YALL).reshape(256, RHS), ("x",)).reshape(128, 8, RHS)

    narrow = combine(root_tiles, term, root_block)
    forward = narrow.astype(F32) + other_core(narrow).astype(F32)
    forward = summed(gather(forward.astype(BF16), Z))
    root_scaled = pivot_solve(forward, dinv_rows, joined_rows).astype(BF16)
    back = transposed_product(root_block[:, :192], root_scaled).astype(BF16)
    back = summed(exchange(back.reshape(4, 48, RHS), ("x",))).astype(BF16)
    root_part = summed(gather(back, YALL)).astype(BF16)
    root_full = both_cores(gather(root_part, ZX)).reshape(16, ROOT_TILES, 8, RHS)
    root_full = root_full.transpose(1, 0, 2, 3).reshape(ROOT_ROWS, RHS)
    root_own = lax.dynamic_slice_in_dim(root_full, lax.axis_index(AXES) * 6, 6, 0)

    tile_ids = lax.dynamic_index_in_dim(root_tiles, lax.axis_index("p"), 0, keepdims=False)
    onehot = (tile_ids[:, None] == jnp.arange(ROOT_TILES, dtype=jnp.int32)[None, :]).astype(BF16)
    tile_values = jnp.einsum(
        "kt,tar->kar", onehot, root_full.reshape(ROOT_TILES, TILE, RHS), preferred_element_type=F32
    )
    tile_values = tile_values.astype(BF16).reshape(LEAF_TILES * TILE, RHS)
    coupling = transposed_product(update, tile_values)
    leaf_joined = jnp.repeat(leaf_doff[0] * leaf_pairs[0].astype(F32), 2)[:, None]
    scaled = pivot_solve(leaf_forward.astype(F32), leaf_dinv[0][:, None], leaf_joined)
    leaf_vector = (scaled - coupling).astype(BF16)
    vector = gather(leaf_vector, CX).reshape(512, RHS)
    back_leaf = transposed_product(blocks, vector)
    back_leaf = with_layout_constraint(back_leaf, Layout(major_to_minor=(0, 1))).astype(BF16)
    leaf_solution = summed(exchange(back_leaf.reshape(16, 64, RHS), YZ)).astype(BF16)
    return (leaf_solution[None], root_own)


def solution(mesh):
    fine = Mesh(mesh.devices.reshape(SIZES), AXES)
    in_specs = (
        P(LEAF, NODE, None),
        P(LEAF, NODE, None),
        P(LEAF, None, NODE),
        P(),
        P(LEAF, NODE),
        P(LEAF, NODE),
        P(LEAF, NODE),
        P(AXES, None),
        P(AXES, None),
        P(AXES),
        P(AXES),
        P(AXES),
    )
    out_specs = (P(LEAF, NODE, None), P(AXES, None))

    return jax.shard_map(
        on_device, mesh=fine, in_specs=in_specs, out_specs=out_specs, check_vma=False
    )
```

```python
import jax
import jax.numpy as jnp
from jax import lax
from jax.experimental import pallas as pl
from jax.experimental.pallas import tpu as pltpu
from jax.sharding import Mesh
from jax.sharding import PartitionSpec as P

LEAVES = 4
ROOT_TILES = 24
LEAF_TILES = 12
TILE = 128
RHS = 128
ROOT_ROWS = ROOT_TILES * TILE

AXES = ("p", "yl", "zl", "c", "zh", "x")
SIZES = (4, 2, 4, 2, 2, 4)
LEAF = ("p", "yl", "zl", "c")
NODE = ("zh", "x")
CX = ("c", "x")
YZ = ("yl", "zl", "zh")
YALL = ("p", "yl")
Z = ("zl", "zh")
ZX = ("zl", "zh", "x")

F32 = jnp.float32
BF16 = jnp.bfloat16


def exchange(blocks, axes):
    return lax.all_to_all(blocks, axes, 0, 0)


def gather(value, axes):
    count = 1
    for axis in axes:
        count *= lax.axis_size(axis)
    return exchange(jnp.broadcast_to(value[None], (count,) + value.shape), axes)


def summed(blocks):
    return jnp.sum(blocks.astype(F32), axis=0)


SCALARS = pl.BlockSpec(memory_space=pltpu.SMEM)
VECTORS = pl.BlockSpec(memory_space=pltpu.VMEM)


def split_columns_kernel(source_ref, out_ref):
    lane = lax.broadcasted_iota(jnp.int32, (64, TILE), 1)
    low = lane < 64
    for m in range(8):
        for core in range(2):
            for xh in range(2):
                first = ((m * 2 + core) * 2) * 2 + xh
                second = first + 2
                a = source_ref[:, first * TILE : (first + 1) * TILE].astype(F32)
                b = source_ref[:, second * TILE : (second + 1) * TILE].astype(F32)
                even = jnp.where(low, a, pltpu.roll(b, 64, 1))
                odd = jnp.where(low, pltpu.roll(a, 64, 1), b)
                place = slice(m * TILE, (m + 1) * TILE)
                out_ref[core * 4 + xh * 2, :, place] = even.astype(BF16)
                out_ref[core * 4 + xh * 2 + 1, :, place] = odd.astype(BF16)


def split_columns(factor_rows):
    return pl.pallas_call(
        split_columns_kernel,
        out_shape=jax.ShapeDtypeStruct((8, 64, 1024), BF16),
    )(factor_rows)


def combine_kernel(tiles_ref, terms_ref, block_ref, wide_ref, narrow_ref, total_ref):
    for y in range(8):
        for j in range(3):
            total_ref[3 * y + j] = -terms_ref[15 * y + 12 + j].astype(F32)
        total_ref[ROOT_TILES + y] = jnp.zeros((8, RHS), F32)
    for p in range(LEAVES):
        for k in range(LEAF_TILES):
            tile = tiles_ref[p, k]
            term = terms_ref[30 * p + k].astype(F32) + terms_ref[30 * p + 15 + k].astype(F32)
            total_ref[tile] = total_ref[tile] + term
    reduced = (-total_ref[...]).reshape(256, RHS).astype(BF16)
    product = jnp.dot(block_ref[...], reduced, preferred_element_type=F32)
    wide_ref[...] = product
    narrow_ref[...] = product.astype(BF16)


def combine(root_tiles, terms, block):
    return pl.pallas_call(
        combine_kernel,
        out_shape=(
            jax.ShapeDtypeStruct((TILE, RHS), F32),
            jax.ShapeDtypeStruct((TILE, RHS), BF16),
        ),
        in_specs=[SCALARS, VECTORS, VECTORS],
        out_specs=(VECTORS, VECTORS),
        scratch_shapes=[pltpu.VMEM((ROOT_TILES + 8, 8, RHS), F32)],
    )(root_tiles, terms, block)


def granule_columns_kernel(dinv_ref, doff_ref, pairs_ref, source_ref, out_ref):
    lane = lax.broadcasted_iota(jnp.int32, (6, TILE), 1)
    slot = lane // 8
    tiles = [source_ref[:, t * TILE : (t + 1) * TILE].astype(F32) for t in range(ROOT_TILES)]
    row = lax.broadcasted_iota(jnp.int32, (6, TILE), 0)
    diagonal = jnp.zeros((6, TILE), F32)
    joined = jnp.zeros((6, TILE), F32)
    for i in range(6):
        diagonal = jnp.where(row == i, dinv_ref[i], diagonal)
        both = doff_ref[i // 2] * pairs_ref[i // 2].astype(F32)
        joined = jnp.where(row == i, both, joined)
    spare = jnp.zeros((6, TILE), F32)
    for j, part in enumerate(parts_of(diagonal) + parts_of(joined)):
        spare = jnp.where(lane == 64 + j, part, spare)
    out_ref[...] = jnp.zeros_like(out_ref)
    for a in range(16):
        first = spare
        second = spare
        for t in range(16):
            first = jnp.where(slot == t, pltpu.roll(tiles[t], (t - a) * 8 % TILE, 1), first)
        for t in range(8):
            second = jnp.where(slot == t, pltpu.roll(tiles[16 + t], (t - a) * 8 % TILE, 1), second)
        out_ref[a, 0, :6] = first.astype(BF16)
        out_ref[a, 1, :6] = second.astype(BF16)


def granule_columns(dinv, doff, pairs, rows):
    return pl.pallas_call(
        granule_columns_kernel,
        out_shape=jax.ShapeDtypeStruct((16, 2, 8, TILE), BF16),
        in_specs=[SCALARS, SCALARS, SCALARS, VECTORS],
        out_specs=VECTORS,
    )(dinv, doff, pairs, rows)


def parts_of(value):
    high = value.astype(BF16).astype(F32)
    rest = value - high
    middle = rest.astype(BF16).astype(F32)
    low = (rest - middle).astype(BF16).astype(F32)
    return [high, middle, low]


def pivot_solve(values, diagonal, joined):
    length = values.shape[0]
    halves = values.reshape(length // 2, 2, values.shape[1])
    swapped = halves[:, ::-1, :].reshape(length, values.shape[1])
    return diagonal * values + joined * swapped


def other_core(value):
    return lax.ppermute(value, "c", [(0, 1), (1, 0)])


def both_cores(value):
    other = other_core(value)
    first = lax.axis_index("c") == 0
    return jnp.where(first, jnp.stack([value, other]), jnp.stack([other, value]))


def gather_leaf_rhs(value):
    def doubled(held, axis, mask, low, place):
        pairs = [(i, i ^ mask) for i in range(lax.axis_size(axis))]
        other = lax.ppermute(held, axis, pairs)
        return jnp.where(low, jnp.stack([held, other], place), jnp.stack([other, held], place))

    zl = lax.axis_index("zl")
    held = doubled(value, "zh", 1, lax.axis_index("zh") == 0, 0)
    held = doubled(held, "zl", 2, zl < 2, 0)
    held = doubled(held, "zl", 1, zl % 2 == 0, 1)
    held = doubled(held, "yl", 1, lax.axis_index("yl") == 0, 0)
    return held.reshape(1024, RHS)


def transposed_product(matrix, vector):
    return lax.dot_general(
        matrix, vector, (((0,), (0,)), ((), ())), preferred_element_type=F32
    )


def xred(term):
    return gather(term, ("x",))


def on_device(
    leaf_rhs,
    leaf_inverse,
    leaf_update,
    root_tiles,
    leaf_dinv,
    leaf_doff,
    leaf_pairs,
    root_rhs,
    root_inverse,
    root_dinv,
    root_doff,
    root_pairs,
):
    blocks = exchange(split_columns(leaf_inverse[0]), CX).reshape(512, 1024)
    rhs_part = gather_leaf_rhs(leaf_rhs[0])
    partial = jnp.dot(blocks, rhs_part, preferred_element_type=F32).astype(BF16)
    update = leaf_update[0]
    at = jnp.arange(16 * 24, dtype=jnp.int32)
    partial, late_update, at = lax.optimization_barrier((partial, update, at))
    partial = exchange(partial.reshape(8, 64, RHS), CX)
    leaf_forward = summed(partial).astype(BF16)

    root_block = granule_columns(root_dinv, root_doff, root_pairs, root_inverse)

    ordered = late_update.reshape(12, 16, 8, 64).transpose(1, 0, 2, 3).reshape(16, 96, 64)
    row = TILE * (3 * lax.axis_index(YALL) + at // 8 % 3) + 8 * (at // 24) + at % 8
    row = row - 6 * lax.axis_index(AXES)
    select = (row[:, None] == jnp.arange(8, dtype=jnp.int32)[None, :]) & (row < 6)[:, None]
    select = select.astype(BF16).reshape(16, 24, 8)
    left = jnp.concatenate(
        [jnp.pad(ordered, ((0, 0), (0, 0), (0, 8))), jnp.pad(select, ((0, 0), (0, 0), (64, 0)))], 1
    ).reshape(1920, 72)
    right = jnp.concatenate([leaf_forward, jnp.pad(root_rhs, ((0, 2), (0, 0)))], 0)
    term = jnp.dot(left, right, preferred_element_type=F32).astype(BF16)
    term = jnp.concatenate([term.reshape(2, 8, 120, RHS), root_block.reshape(2, 8, 16, RHS)], 2)
    term = exchange(term.reshape(2, 1088, RHS), ("c",)).reshape(2, 8, 136, RHS)
    root_block = term[:, :, 120:].transpose(1, 0, 2, 3).reshape(8, 32, RHS)
    term = summed(term[:, :, :120]).astype(BF16)
    term = exchange(jnp.concatenate([term, root_block], 1), Z)
    root_block = term[:, 120:].reshape(8, 2, 2, 8, RHS).transpose(0, 1, 3, 2, 4).reshape(128, 2 * TILE)
    pivots = root_block[:, 192:198].astype(F32)
    dinv_rows = pivots[:, 0:1] + pivots[:, 1:2] + pivots[:, 2:3]
    joined_rows = pivots[:, 3:4] + pivots[:, 4:5] + pivots[:, 5:6]
    term = summed(term[:, :120]).astype(BF16)
    term, root_block, dinv_rows, joined_rows = lax.optimization_barrier(
        (xred(term), root_block, dinv_rows, joined_rows)
    )
    term = summed(term).astype(BF16)
    term = gather(term, YALL).reshape(120, 8, RHS)

    wide, narrow = combine(root_tiles, term, root_block)
    forward = wide + other_core(narrow).astype(F32)
    forward = summed(gather(forward.astype(BF16), Z))
    root_scaled = pivot_solve(forward, dinv_rows, joined_rows).astype(BF16)
    back = transposed_product(root_block[:, :192], root_scaled).astype(BF16)
    back = summed(exchange(back.reshape(4, 48, RHS), ("x",))).astype(BF16)
    root_part = summed(gather(back, YALL)).astype(BF16)
    root_full = both_cores(gather(root_part, ZX)).reshape(16, ROOT_TILES, 8, RHS)
    root_full = root_full.transpose(1, 0, 2, 3).reshape(ROOT_ROWS, RHS)
    root_own = lax.dynamic_slice_in_dim(root_full, lax.axis_index(AXES) * 6, 6, 0)

    tile_ids = lax.dynamic_index_in_dim(root_tiles, lax.axis_index("p"), 0, keepdims=False)
    onehot = (tile_ids[:, None] == jnp.arange(ROOT_TILES, dtype=jnp.int32)[None, :]).astype(BF16)
    tile_values = jnp.einsum(
        "kt,tar->kar", onehot, root_full.reshape(ROOT_TILES, TILE, RHS), preferred_element_type=F32
    )
    tile_values = tile_values.astype(BF16).reshape(LEAF_TILES * TILE, RHS)
    coupling = transposed_product(update, tile_values)
    leaf_joined = jnp.repeat(leaf_doff[0] * leaf_pairs[0].astype(F32), 2)[:, None]
    scaled = pivot_solve(leaf_forward.astype(F32), leaf_dinv[0][:, None], leaf_joined)
    leaf_vector = (scaled - coupling).astype(BF16)
    vector = gather(leaf_vector, CX).reshape(512, RHS)
    back_leaf = transposed_product(blocks, vector).astype(BF16)
    leaf_solution = summed(exchange(back_leaf.reshape(16, 64, RHS), YZ)).astype(BF16)
    return (leaf_solution[None], root_own)


def solution(mesh):
    fine = Mesh(mesh.devices.reshape(SIZES), AXES)
    in_specs = (
        P(LEAF, NODE, None),
        P(LEAF, NODE, None),
        P(LEAF, None, NODE),
        P(),
        P(LEAF, NODE),
        P(LEAF, NODE),
        P(LEAF, NODE),
        P(AXES, None),
        P(AXES, None),
        P(AXES),
        P(AXES),
        P(AXES),
    )
    out_specs = (P(LEAF, NODE, None), P(AXES, None))

    return jax.shard_map(
        on_device, mesh=fine, in_specs=in_specs, out_specs=out_specs, check_vma=False
    )
```

```python
import jax
import jax.numpy as jnp
from jax import lax
from jax.experimental import pallas as pl
from jax.experimental.pallas import tpu as pltpu
from jax.sharding import Mesh
from jax.sharding import PartitionSpec as P

LEAVES = 4
ROOT_TILES = 24
LEAF_TILES = 12
TILE = 128
RHS = 128
ROOT_ROWS = ROOT_TILES * TILE

AXES = ("p", "yl", "zl", "c", "zh", "x")
SIZES = (4, 2, 4, 2, 2, 4)
LEAF = ("p", "yl", "zl", "c")
NODE = ("zh", "x")
CX = ("c", "x")
YZ = ("yl", "zl", "zh")
YALL = ("p", "yl")
Z = ("zl", "zh")
ZX = ("zl", "zh", "x")

F32 = jnp.float32
BF16 = jnp.bfloat16


def exchange(blocks, axes):
    return lax.all_to_all(blocks, axes, 0, 0)


def gather(value, axes):
    count = 1
    for axis in axes:
        count *= lax.axis_size(axis)
    return exchange(jnp.broadcast_to(value[None], (count,) + value.shape), axes)


def summed(blocks):
    return jnp.sum(blocks.astype(F32), axis=0)


SCALARS = pl.BlockSpec(memory_space=pltpu.SMEM)
VECTORS = pl.BlockSpec(memory_space=pltpu.VMEM)


def split_columns_kernel(source_ref, out_ref):
    lane = lax.broadcasted_iota(jnp.int32, (64, TILE), 1)
    low = lane < 64
    for m in range(8):
        for core in range(2):
            for xh in range(2):
                first = ((m * 2 + core) * 2) * 2 + xh
                second = first + 2
                a = source_ref[:, first * TILE : (first + 1) * TILE].astype(F32)
                b = source_ref[:, second * TILE : (second + 1) * TILE].astype(F32)
                even = jnp.where(low, a, pltpu.roll(b, 64, 1))
                odd = jnp.where(low, pltpu.roll(a, 64, 1), b)
                place = slice(m * TILE, (m + 1) * TILE)
                out_ref[core * 4 + xh * 2, :, place] = even.astype(BF16)
                out_ref[core * 4 + xh * 2 + 1, :, place] = odd.astype(BF16)


def split_columns(factor_rows):
    return pl.pallas_call(
        split_columns_kernel,
        out_shape=jax.ShapeDtypeStruct((8, 64, 1024), BF16),
    )(factor_rows)


def combine_kernel(tiles_ref, terms_ref, block_ref, out_ref, total_ref):
    for y in range(8):
        for j in range(3):
            total_ref[3 * y + j] = -terms_ref[15 * y + 12 + j].astype(F32)
        total_ref[ROOT_TILES + y] = jnp.zeros((8, RHS), F32)
    for p in range(LEAVES):
        for k in range(LEAF_TILES):
            tile = tiles_ref[p, k]
            term = terms_ref[30 * p + k].astype(F32) + terms_ref[30 * p + 15 + k].astype(F32)
            total_ref[tile] = total_ref[tile] + term
    reduced = (-total_ref[...]).reshape(256, RHS).astype(BF16)
    product = jnp.dot(block_ref[...], reduced, preferred_element_type=F32)
    out_ref[...] = product.astype(BF16)


def combine(root_tiles, terms, block):
    return pl.pallas_call(
        combine_kernel,
        out_shape=jax.ShapeDtypeStruct((TILE, RHS), BF16),
        in_specs=[SCALARS, VECTORS, VECTORS],
        out_specs=VECTORS,
        scratch_shapes=[pltpu.VMEM((ROOT_TILES + 8, 8, RHS), F32)],
    )(root_tiles, terms, block)


def granule_columns_kernel(dinv_ref, doff_ref, pairs_ref, source_ref, out_ref):
    lane = lax.broadcasted_iota(jnp.int32, (6, TILE), 1)
    slot = lane // 8
    tiles = [source_ref[:, t * TILE : (t + 1) * TILE].astype(F32) for t in range(ROOT_TILES)]
    row = lax.broadcasted_iota(jnp.int32, (6, TILE), 0)
    diagonal = jnp.zeros((6, TILE), F32)
    joined = jnp.zeros((6, TILE), F32)
    for i in range(6):
        diagonal = jnp.where(row == i, dinv_ref[i], diagonal)
        both = doff_ref[i // 2] * pairs_ref[i // 2].astype(F32)
        joined = jnp.where(row == i, both, joined)
    spare = jnp.zeros((6, TILE), F32)
    for j, part in enumerate(parts_of(diagonal) + parts_of(joined)):
        spare = jnp.where(lane == 64 + j, part, spare)
    out_ref[...] = jnp.zeros_like(out_ref)
    for a in range(16):
        first = spare
        second = spare
        for t in range(16):
            first = jnp.where(slot == t, pltpu.roll(tiles[t], (t - a) * 8 % TILE, 1), first)
        for t in range(8):
            second = jnp.where(slot == t, pltpu.roll(tiles[16 + t], (t - a) * 8 % TILE, 1), second)
        out_ref[a, 0, :6] = first.astype(BF16)
        out_ref[a, 1, :6] = second.astype(BF16)


def granule_columns(dinv, doff, pairs, rows):
    return pl.pallas_call(
        granule_columns_kernel,
        out_shape=jax.ShapeDtypeStruct((16, 2, 8, TILE), BF16),
        in_specs=[SCALARS, SCALARS, SCALARS, VECTORS],
        out_specs=VECTORS,
    )(dinv, doff, pairs, rows)


def parts_of(value):
    high = value.astype(BF16).astype(F32)
    rest = value - high
    middle = rest.astype(BF16).astype(F32)
    low = (rest - middle).astype(BF16).astype(F32)
    return [high, middle, low]


def pivot_solve(values, diagonal, joined):
    length = values.shape[0]
    halves = values.reshape(length // 2, 2, values.shape[1])
    swapped = halves[:, ::-1, :].reshape(length, values.shape[1])
    return diagonal * values + joined * swapped


def other_core(value):
    return lax.ppermute(value, "c", [(0, 1), (1, 0)])


def both_cores(value):
    other = other_core(value)
    first = lax.axis_index("c") == 0
    return jnp.where(first, jnp.stack([value, other]), jnp.stack([other, value]))


def gather_leaf_rhs(value):
    def doubled(held, axis, mask, low, place):
        pairs = [(i, i ^ mask) for i in range(lax.axis_size(axis))]
        other = lax.ppermute(held, axis, pairs)
        return jnp.where(low, jnp.stack([held, other], place), jnp.stack([other, held], place))

    zl = lax.axis_index("zl")
    held = doubled(value, "zh", 1, lax.axis_index("zh") == 0, 0)
    held = doubled(held, "zl", 2, zl < 2, 0)
    held = doubled(held, "zl", 1, zl % 2 == 0, 1)
    held = doubled(held, "yl", 1, lax.axis_index("yl") == 0, 0)
    return held.reshape(1024, RHS)


def transposed_product(matrix, vector):
    return lax.dot_general(
        matrix, vector, (((0,), (0,)), ((), ())), preferred_element_type=F32
    )


def xred(term):
    return gather(term, ("x",))


def on_device(
    leaf_rhs,
    leaf_inverse,
    leaf_update,
    root_tiles,
    leaf_dinv,
    leaf_doff,
    leaf_pairs,
    root_rhs,
    root_inverse,
    root_dinv,
    root_doff,
    root_pairs,
):
    blocks = exchange(split_columns(leaf_inverse[0]), CX).reshape(512, 1024)
    rhs_part = gather_leaf_rhs(leaf_rhs[0])
    partial = jnp.dot(blocks, rhs_part, preferred_element_type=F32).astype(BF16)
    update = leaf_update[0]
    at = jnp.arange(16 * 24, dtype=jnp.int32)
    partial, late_update, at = lax.optimization_barrier((partial, update, at))
    partial = exchange(partial.reshape(8, 64, RHS), CX)
    leaf_forward = summed(partial).astype(BF16)

    root_block = granule_columns(root_dinv, root_doff, root_pairs, root_inverse)

    ordered = late_update.reshape(12, 16, 8, 64).transpose(1, 0, 2, 3).reshape(16, 96, 64)
    row = TILE * (3 * lax.axis_index(YALL) + at // 8 % 3) + 8 * (at // 24) + at % 8
    row = row - 6 * lax.axis_index(AXES)
    select = (row[:, None] == jnp.arange(8, dtype=jnp.int32)[None, :]) & (row < 6)[:, None]
    select = select.astype(BF16).reshape(16, 24, 8)
    left = jnp.concatenate(
        [jnp.pad(ordered, ((0, 0), (0, 0), (0, 8))), jnp.pad(select, ((0, 0), (0, 0), (64, 0)))], 1
    ).reshape(1920, 72)
    right = jnp.concatenate([leaf_forward, jnp.pad(root_rhs, ((0, 2), (0, 0)))], 0)
    term = jnp.dot(left, right, preferred_element_type=F32).astype(BF16)
    term = jnp.concatenate([term.reshape(2, 8, 120, RHS), root_block.reshape(2, 8, 16, RHS)], 2)
    term = exchange(term.reshape(2, 1088, RHS), ("c",)).reshape(2, 8, 136, RHS)
    root_block = term[:, :, 120:].transpose(1, 0, 2, 3).reshape(8, 32, RHS)
    term = summed(term[:, :, :120]).astype(BF16)
    term = exchange(jnp.concatenate([term, root_block], 1), Z)
    root_block = term[:, 120:].reshape(8, 2, 2, 8, RHS).transpose(0, 1, 3, 2, 4).reshape(128, 2 * TILE)
    pivots = root_block[:, 192:198].astype(F32)
    dinv_rows = pivots[:, 0:1] + pivots[:, 1:2] + pivots[:, 2:3]
    joined_rows = pivots[:, 3:4] + pivots[:, 4:5] + pivots[:, 5:6]
    term = summed(term[:, :120]).astype(BF16)
    term, root_block, dinv_rows, joined_rows = lax.optimization_barrier(
        (xred(term), root_block, dinv_rows, joined_rows)
    )
    term = summed(term).astype(BF16)
    term = gather(term, YALL).reshape(120, 8, RHS)

    narrow = combine(root_tiles, term, root_block)
    forward = narrow.astype(F32) + other_core(narrow).astype(F32)
    forward = summed(gather(forward.astype(BF16), Z))
    root_scaled = pivot_solve(forward, dinv_rows, joined_rows).astype(BF16)
    back = transposed_product(root_block[:, :192], root_scaled).astype(BF16)
    back = summed(exchange(back.reshape(4, 48, RHS), ("x",))).astype(BF16)
    root_part = summed(gather(back, YALL)).astype(BF16)
    root_full = both_cores(gather(root_part, ZX)).reshape(16, ROOT_TILES, 8, RHS)
    root_full = root_full.transpose(1, 0, 2, 3).reshape(ROOT_ROWS, RHS)
    root_own = lax.dynamic_slice_in_dim(root_full, lax.axis_index(AXES) * 6, 6, 0)

    tile_ids = lax.dynamic_index_in_dim(root_tiles, lax.axis_index("p"), 0, keepdims=False)
    onehot = (tile_ids[:, None] == jnp.arange(ROOT_TILES, dtype=jnp.int32)[None, :]).astype(BF16)
    tile_values = jnp.einsum(
        "kt,tar->kar", onehot, root_full.reshape(ROOT_TILES, TILE, RHS), preferred_element_type=F32
    )
    tile_values = tile_values.astype(BF16).reshape(LEAF_TILES * TILE, RHS)
    coupling = transposed_product(update, tile_values)
    leaf_joined = jnp.repeat(leaf_doff[0] * leaf_pairs[0].astype(F32), 2)[:, None]
    scaled = pivot_solve(leaf_forward.astype(F32), leaf_dinv[0][:, None], leaf_joined)
    leaf_vector = (scaled - coupling).astype(BF16)
    vector = gather(leaf_vector, CX).reshape(512, RHS)
    back_leaf = transposed_product(blocks, vector).astype(BF16)
    leaf_solution = summed(exchange(back_leaf.reshape(16, 64, RHS), YZ)).astype(BF16)
    return (leaf_solution[None], root_own)


def solution(mesh):
    fine = Mesh(mesh.devices.reshape(SIZES), AXES)
    in_specs = (
        P(LEAF, NODE, None),
        P(LEAF, NODE, None),
        P(LEAF, None, NODE),
        P(),
        P(LEAF, NODE),
        P(LEAF, NODE),
        P(LEAF, NODE),
        P(AXES, None),
        P(AXES, None),
        P(AXES),
        P(AXES),
        P(AXES),
    )
    out_specs = (P(LEAF, NODE, None), P(AXES, None))

    return jax.shard_map(
        on_device, mesh=fine, in_specs=in_specs, out_specs=out_specs, check_vma=False
    )
```
